256 devices in a mesh: rows: 32 (over x, z), feat: 8 (over y, core).
Axes of the slice: x: 4, y: 4, z: 8, core: 2. Of those that a mesh axis runs over, the one named last changes fastest.
Arguments:
- feature_values: float32 [512, 262144], P('feat', 'rows'), as said below
- hessian_codes: int32 [262144], P(('rows', 'feat')), may hold values from 1024 to 24576
- edge_codes: int32 [512, 256], P('feat'), may hold values from -4096 to 4096, as said below
- cut_ranks: int32 [512, 256], P('feat'), may hold values from 160 to 65632, as said below
Outputs:
- bin_positions: float32 [512, 262144], P(None, ('rows', 'feat'))
The draws below stay inside these ranges and needn't reach their ends.
Inputs may be any that keep to these rules, and one draw needn't show every extreme that they name: `feature_values`: every value lies strictly between its feature's first and last grid edge, and each grid cell between two consecutive edges holds at least 514 rows of that feature. `edge_codes`: strictly increasing along each feature; every feature's first code is -4096 and its last 4096. `cut_ranks`: strictly increasing along each feature; the k-th cut's rank (counting from 0) lies within 96 of 256 * (k + 1).
All inputs are finite; a program needn't handle non-finite values.
Results may differ from the reference program's by a relative error of at most 0.0003.
Values sent between devices are 32-bit elements; how exact they have to be, the bound alone decides.
No kernel may reach another device: no remote copies, remote signals or barrier semaphores. Data moves between devices by JAX's collectives and lax.ppermute only.
A program may use at most 64 MiB of HBM per device.

```python
import jax
import jax.numpy as jnp
from jax import lax

F = 512
G = 256
K = 256
ROWS = 262144


def edge_table(key):
    table_key = jax.random.fold_in(key, 11)
    spacing = 2048 // G
    steps_drawn = jax.random.randint(table_key, (F, G - 3), spacing, 3 * spacing + 1, dtype=jnp.int32)
    running = jnp.cumsum(steps_drawn, axis=1)
    anchor = -(running[:, -1:] // 2)
    interior = jnp.concatenate([anchor, anchor + running], axis=1)
    low_end = jnp.full((F, 1), -4096, dtype=jnp.int32)
    high_end = jnp.full((F, 1), 4096, dtype=jnp.int32)
    return jnp.concatenate([low_end, interior, high_end], axis=1).astype(jnp.int32)


def draw_edge_codes(key, part):
    return edge_table(key)


def draw_feature_values(key, part):
    grid_edges = edge_table(key).astype(jnp.float32) / 256.0
    row_index = jnp.arange(ROWS, dtype=jnp.int32)[None, :]
    feat_index = jnp.arange(F, dtype=jnp.int32)[:, None]
    cell_index = (row_index // 2 + 37 * feat_index) % (G - 1) + 1
    low_edge = jnp.take_along_axis(grid_edges, cell_index - 1, axis=1)
    high_edge = jnp.take_along_axis(grid_edges, cell_index, axis=1)
    first_key, second_key, third_key, fourth_key = jax.random.split(jax.random.fold_in(key, 23), 4)
    fraction = jax.random.uniform(first_key, (F, ROWS), jnp.float32, 0.1, 0.9)
    spread_part = low_edge + fraction * (high_edge - low_edge)
    centers = jax.random.uniform(second_key, (F, 8), jnp.float32, -3.0, 3.0)
    jitter = jnp.clip(0.01 * jax.random.normal(fourth_key, (F, ROWS), jnp.float32), -0.05, 0.05)
    clump_pick = jax.random.randint(third_key, (F, ROWS), 0, 8, dtype=jnp.int32)
    clump_part = jnp.take_along_axis(centers, clump_pick, axis=1) + jitter
    return jnp.where(row_index % 2 == 0, spread_part, clump_part).astype(jnp.float32)


def draw_hessian_codes(key, part):
    draw_key = jax.random.fold_in(key, 31)
    row_index = jnp.arange(ROWS, dtype=jnp.int32)
    base_codes = jax.random.randint(draw_key, (ROWS,), 1024, 8193, dtype=jnp.int32)
    base_codes = jnp.where(row_index == 0, 1024, jnp.where(row_index == ROWS - 1, 8192, base_codes))
    level_index = row_index * 16 // ROWS
    return (base_codes * (15 + 2 * level_index) // 15).astype(jnp.int32)


def draw_cut_ranks(key, part):
    jitter = jax.random.randint(jax.random.fold_in(key, 41), (F, K), -96, 97, dtype=jnp.int32)
    feat_index = jnp.arange(F, dtype=jnp.int32)[:, None]
    cut_index = jnp.arange(K, dtype=jnp.int32)[None, :]
    jitter = jnp.where((feat_index == 0) & (cut_index == 0), -96, jitter)
    jitter = jnp.where((feat_index == 0) & (cut_index == K - 1), 96, jitter)
    return (256 * (cut_index + 1) + jitter).astype(jnp.int32)


def setup_inputs(seed: int = 0) -> dict:
    keys = jax.random.split(jax.random.key(seed), 5)
    feature_values = draw_feature_values(jax.random.fold_in(keys[4], 71), 0)
    hessian_codes = draw_hessian_codes(jax.random.fold_in(keys[4], 71), 0)
    edge_codes = draw_edge_codes(jax.random.fold_in(keys[4], 71), 0)
    cut_ranks = draw_cut_ranks(jax.random.fold_in(keys[4], 71), 0)
    return dict(feature_values=feature_values, hessian_codes=hessian_codes, edge_codes=edge_codes, cut_ranks=cut_ranks)


rank_step = 256.0


def mass_table(values, grid_edges, hess_slab):
    feature_count = values.shape[0]
    grid_points = grid_edges.shape[1]
    grid_slot = jax.vmap(lambda edge_row, value_row: jnp.searchsorted(edge_row, value_row, side="right"))(grid_edges, values).astype(jnp.int32)
    offsets = (jnp.arange(feature_count, dtype=jnp.int32) * grid_points)[:, None]
    flat_ids = (grid_slot + offsets).reshape(-1)
    weighted = jnp.broadcast_to(hess_slab[None, :], values.shape).reshape(-1)
    counts = jax.ops.segment_sum(weighted, flat_ids, num_segments=feature_count * grid_points)
    return jnp.cumsum(counts.reshape(feature_count, grid_points), axis=1)


def invert_cdf(mass_row, edge_row, targets):
    crossed = jnp.sum((mass_row[None, :] <= targets[:, None]).astype(jnp.int32), axis=1)
    low_mass = jnp.take(mass_row, crossed - 1)
    high_mass = jnp.take(mass_row, crossed)
    low_edge = jnp.take(edge_row, crossed - 1)
    high_edge = jnp.take(edge_row, crossed)
    return low_edge + (targets - low_mass) / (high_mass - low_mass) * (high_edge - low_edge)


def bucketize(values, cut_knots):
    def one_row(knot_row, value_row):
        knot_below = jnp.searchsorted(knot_row, value_row, side="right").astype(jnp.int32) - 1
        low_knot = jnp.take(knot_row, knot_below)
        high_knot = jnp.take(knot_row, knot_below + 1)
        return knot_below.astype(jnp.float32) + (value_row - low_knot) / (high_knot - low_knot)
    return jax.vmap(one_row)(cut_knots, values)


def reference(feature_values, hessian_codes, edge_codes, cut_ranks):
    hess_slab = hessian_codes.astype(jnp.float32) * (1.0 / 65536.0)
    total_mass = jnp.sum(hess_slab)
    grid_edges = edge_codes.astype(jnp.float32) / 256.0

    def one_feature(feature_items):
        value_row, edge_row, rank_row = feature_items
        mass_row = mass_table(value_row[None, :], edge_row[None, :], hess_slab)[0]
        targets = rank_row.astype(jnp.float32) / (rank_step * (K + 1)) * total_mass
        cut_values = invert_cdf(mass_row, edge_row, targets)
        cut_knots = jnp.concatenate([edge_row[:1], cut_values, edge_row[-1:]])
        return bucketize(value_row[None, :], cut_knots[None, :])[0]

    return lax.map(one_feature, (feature_values, grid_edges, cut_ranks))
```

```python
import jax
import jax.numpy as jnp
from jax import lax
from jax.experimental import pallas as pl
from jax.experimental.pallas import tpu as pltpu
from jax.sharding import PartitionSpec as P

LANES = 128


def lane_take(table, index):
    return jnp.take_along_axis(table, index, axis=1, mode="promise_in_bounds")


def pick_columns(wide, index):
    low = lane_take(wide[:, :LANES], index & (LANES - 1))
    high = lane_take(wide[:, LANES:], index & (LANES - 1))
    return jnp.where(index < LANES, low, high)


def lane_iota(shape):
    return lax.broadcasted_iota(jnp.int32, shape, 1)


def search_pair(even, middle, value):
    base = jnp.where(value >= middle, 64, 0)
    for step in (32, 16, 8, 4, 2, 1):
        probe = base + step
        base = jnp.where(value >= lane_take(even, probe), probe, base)
    return base


def mass_kernel(codes_ref, hess_ref, values_ref, mass_ref, a_ref, b_ref, w_ref):
    feats, rows = values_ref.shape
    shape = (feats, LANES)
    lane = lane_iota(shape)
    feat = lax.broadcasted_iota(jnp.int32, shape, 0)
    edges = codes_ref[...].astype(jnp.float32) * (1.0 / 256.0)
    even = pick_columns(edges, 2 * lane)
    odd = pick_columns(edges, 2 * lane + 1)
    middle = jnp.broadcast_to(even[:, 64:65], shape)

    @pl.when(pl.program_id(0) == 0)
    def _():
        scaled = jnp.broadcast_to(hess_ref[...] * 65536.0, (feats, rows))
        high = jnp.floor(scaled * (1.0 / 256.0))
        w_ref[0] = high.astype(jnp.bfloat16)
        w_ref[1] = (scaled - high * 256.0).astype(jnp.bfloat16)

    def chunk(step, carry):
        for part in range(4):
            at = pl.multiple_of(step * (4 * LANES) + part * LANES, LANES)
            value = values_ref[:, pl.ds(at, LANES)]
            pair = search_pair(even, middle, value)
            top = (pair >> 3).astype(jnp.float32).astype(jnp.bfloat16)
            bit = jnp.where(value >= lane_take(odd, pair), 1, 0)
            low = (2 * (pair & 7) + bit).astype(jnp.float32).astype(jnp.bfloat16)
            w_high = w_ref[0, :, pl.ds(at, LANES)]
            w_low = w_ref[1, :, pl.ds(at, LANES)]
            zero = jnp.zeros(shape, jnp.bfloat16)
            one = jnp.ones(shape, jnp.bfloat16)
            for k in range(16):
                hit = top == k
                a_ref[k * feats:(k + 1) * feats, pl.ds(at, LANES)] = jnp.where(hit, w_high, zero)
                a_ref[(16 + k) * feats:(17 + k) * feats, pl.ds(at, LANES)] = jnp.where(hit, w_low, zero)
                b_ref[k * feats:(k + 1) * feats, pl.ds(at, LANES)] = jnp.where(low <= k, one, zero)
        return carry

    lax.fori_loop(0, rows // (4 * LANES), chunk, 0)
    sums = lax.dot_general(a_ref[...], b_ref[...], (((1,), (1,)), ((), ())), preferred_element_type=jnp.float32)
    half = 16 * feats
    table = (sums[:half] * 256.0 + sums[half:]) * (1.0 / 65536.0)
    for parity in range(2):
        point = 2 * lane + parity - 1
        column = (point & 7) * feats + feat
        result = jnp.zeros(shape, jnp.float32)
        before = jnp.zeros(shape, jnp.float32)
        for k in range(16):
            block = table[k * feats:(k + 1) * feats]
            here = jnp.where((point & 15) < 8, lane_take(block[:, :LANES], column), lane_take(block[:, LANES:], column))
            result = jnp.where((point >> 4) == k, before + here, result)
            before = before + lane_take(block[:, LANES:], 7 * feats + feat)
        mass_ref[:, parity * LANES:(parity + 1) * LANES] = result


def local_mass(values, edge_codes, hess):
    feats, rows = values.shape
    group = 16
    return pl.pallas_call(
        mass_kernel,
        grid=(feats // group,),
        in_specs=[
            pl.BlockSpec((group, 256), lambda i: (i, 0)),
            pl.BlockSpec((1, rows), lambda i: (0, 0)),
            pl.BlockSpec((group, rows), lambda i: (i, 0)),
        ],
        out_specs=pl.BlockSpec((group, 256), lambda i: (i, 0)),
        out_shape=jax.ShapeDtypeStruct((feats, 256), jnp.float32),
        scratch_shapes=[
            pltpu.VMEM((32 * group, rows), jnp.bfloat16),
            pltpu.VMEM((16 * group, rows), jnp.bfloat16),
            pltpu.VMEM((2, group, rows), jnp.bfloat16),
        ],
        compiler_params=pltpu.CompilerParams(vmem_limit_bytes=40 << 20),
    )(edge_codes, hess.reshape(1, rows), values)


def next_even(even, lane, last):
    return jnp.where(lane == LANES - 1, last, lane_take(even, (lane + 1) & (LANES - 1)))


def cuts_kernel(codes_ref, ranks_ref, mass_ref, cuts_ref):
    feats = codes_ref.shape[0]
    shape = (feats, LANES)
    lane = lane_iota(shape)
    edges = codes_ref[...].astype(jnp.float32) * (1.0 / 256.0)
    edge_even = pick_columns(edges, 2 * lane)
    edge_odd = pick_columns(edges, 2 * lane + 1)
    edge_next = lane_take(edge_even, (lane + 1) & (LANES - 1))
    mass_even = mass_ref[:, :LANES]
    mass_odd = mass_ref[:, LANES:]
    mass_next = lane_take(mass_even, (lane + 1) & (LANES - 1))
    middle = jnp.broadcast_to(mass_even[:, 64:65], shape)
    total = jnp.broadcast_to(mass_odd[:, LANES - 1:], shape)
    ranks = ranks_ref[...].astype(jnp.float32)
    for side in range(2):
        order = 2 * lane if side else jnp.where(lane == 0, 255, 2 * lane - 1)
        target = pick_columns(ranks, order) * (1.0 / 65792.0) * total
        pair = search_pair(mass_even, middle, target)
        mid_mass = lane_take(mass_odd, pair)
        mid_edge = lane_take(edge_odd, pair)
        above = target >= mid_mass
        low_mass = jnp.where(above, mid_mass, lane_take(mass_even, pair))
        high_mass = jnp.where(above, lane_take(mass_next, pair), mid_mass)
        low_edge = jnp.where(above, mid_edge, lane_take(edge_even, pair))
        high_edge = jnp.where(above, lane_take(edge_next, pair), mid_edge)
        cuts_ref[:, side * LANES:(side + 1) * LANES] = low_edge + (target - low_mass) / (high_mass - low_mass) * (high_edge - low_edge)


def find_cuts(edge_codes, cut_ranks, mass):
    return pl.pallas_call(
        cuts_kernel,
        out_shape=jax.ShapeDtypeStruct(mass.shape, jnp.float32),
    )(edge_codes, cut_ranks, mass)


def place_kernel(cuts_ref, values_ref, out_ref):
    feats, rows = values_ref.shape
    shape = (8, LANES)
    lane = lane_iota(shape)
    for group in range(feats // 8):
        some = slice(group * 8, group * 8 + 8)
        raw = cuts_ref[some, :LANES]
        odd = cuts_ref[some, LANES:]
        last = jnp.broadcast_to(raw[:, :1], shape)
        even = jnp.where(lane == 0, -16.0, raw)
        after = next_even(even, lane, last)
        inv_low = 1.0 / (odd - even)
        inv_high = 1.0 / (after - odd)
        inv_last = 1.0 / (16.0 - last)
        middle = jnp.broadcast_to(raw[:, 64:65], shape)

        def chunk(step, carry):
            for part in range(8):
                at = pl.multiple_of(step * (8 * LANES) + part * LANES, LANES)
                value = values_ref[some, pl.ds(at, LANES)]
                pair = search_pair(even, middle, value)
                knot = lane_take(odd, pair)
                slope = jnp.where(value >= knot, lane_take(inv_high, pair), lane_take(inv_low, pair))
                whole = (2 * pair + 1).astype(jnp.float32)
                inside = whole + (value - knot) * slope
                out_ref[some, pl.ds(at, LANES)] = jnp.where(value >= last, 256.0 + (value - last) * inv_last, inside)
            return carry

        lax.fori_loop(0, rows // (8 * LANES), chunk, 0)


def place(cuts, values):
    feats, rows = values.shape
    group = 16 if rows > 1024 else feats
    return pl.pallas_call(
        place_kernel,
        grid=(feats // group,),
        in_specs=[
            pl.BlockSpec((group, 256), lambda i: (i, 0)),
            pl.BlockSpec((group, rows), lambda i: (i, 0)),
        ],
        out_specs=pl.BlockSpec((group, rows), lambda i: (i, 0)),
        out_shape=jax.ShapeDtypeStruct((feats, rows), jnp.float32),
    )(cuts, values)


def swap_rows(array, flip):
    count = lax.axis_size("rows")
    return lax.ppermute(array, "rows", [(i, i ^ flip) for i in range(count)])


def sum_rows(array):
    for flip in (1, 2, 4, 8, 16):
        array = array + swap_rows(array, flip)
    return array


def on_device(feature_values, hessian_codes, edge_codes, cut_ranks):
    hess_own = hessian_codes.astype(jnp.float32) * (1.0 / 65536.0)
    hess_slab = lax.all_gather(hess_own, "feat", axis=0, tiled=True)
    mass = sum_rows(local_mass(feature_values, edge_codes, hess_slab))
    cuts = find_cuts(edge_codes, cut_ranks, mass)
    positions = place(cuts, feature_values)
    return lax.all_to_all(positions, "feat", split_axis=1, concat_axis=0, tiled=True)


def solution(mesh):
    placed = (P("feat", "rows"), P(("rows", "feat")), P("feat", None), P("feat", None))
    return jax.shard_map(
        on_device, mesh=mesh, in_specs=placed, out_specs=P(None, ("rows", "feat")), check_vma=False
    )
```

```python
import jax
import jax.numpy as jnp
from jax import lax
from jax.experimental import pallas as pl
from jax.experimental.pallas import tpu as pltpu
from jax.sharding import PartitionSpec as P

LANES = 128
FEATS = 16
DEPTH = 4
SPAN = 2048


def in_vmem(count):
    return [pl.BlockSpec(memory_space=pltpu.VMEM)] * count


def lane_take(table, index):
    return jnp.take_along_axis(table, index, axis=1, mode="promise_in_bounds")


def pick_columns(wide, index):
    low = lane_take(wide[:, :LANES], index & (LANES - 1))
    high = lane_take(wide[:, LANES:], index & (LANES - 1))
    return jnp.where(index < LANES, low, high)


def lane_iota(shape):
    return lax.broadcasted_iota(jnp.int32, shape, 1)


def choose(marks, low, high, masks):
    middle = (low + high) // 2
    if not masks:
        return marks[middle]
    upper = choose(marks, middle, high, masks[1:])
    return jnp.where(masks[0], upper, choose(marks, low, middle, masks[1:]))


def spread(even):
    return {i: jnp.broadcast_to(even[:, i : i + 1], even.shape) for i in range(128 >> DEPTH, 128, 128 >> DEPTH)}


def search_pairs(tables, values):
    masks = [[] for _ in values]
    for _ in range(DEPTH):
        for (_, marks), mask, value in zip(tables, masks, values):
            mask.append(value >= choose(marks, 0, LANES, mask))
    bases = []
    for mask in masks:
        base = jnp.where(mask[0], 64, 0)
        for level in range(1, DEPTH):
            base = base + jnp.where(mask[level], 64 >> level, 0)
        bases.append(base)
    step = 64 >> DEPTH
    while step:
        probes = [base + step for base in bases]
        entries = [lane_take(even, probe) for (even, _), probe in zip(tables, probes)]
        bases = [jnp.where(v >= e, p, b) for v, e, p, b in zip(values, entries, probes, bases)]
        step //= 2
    return bases


def even_odd(codes):
    lane = lane_iota((codes.shape[0], LANES))
    edges = codes.astype(jnp.float32) * (1.0 / 256.0)
    return pick_columns(edges, 2 * lane), pick_columns(edges, 2 * lane + 1)


def slot_kernel(turn, codes_ref, values_ref, top_ref, low_ref):
    rows = values_ref.shape[1]
    width = 32
    group = (lax.axis_index("rows") // 8 + turn) % 4
    tables = []
    for half in range(2):
        at = pl.ds(pl.multiple_of(group * FEATS + 8 * half, 8), 8)
        even, odd = even_odd(codes_ref[at, :])
        tables.append((at, odd, (even, spread(even))))

    def chunk(step, carry):
        columns = [pl.ds(pl.multiple_of((step * width + part) * LANES, LANES), LANES) for part in range(width)]
        tops, lows = [[] for _ in columns], [[] for _ in columns]
        for at, odd, table in tables:
            values = [values_ref[at, column] for column in columns]
            pairs = search_pairs([table] * width, values)
            entries = [lane_take(odd, pair) for pair in pairs]
            for top, low, value, pair, entry in zip(tops, lows, values, pairs, entries):
                top.append((pair >> 3).astype(jnp.float32))
                low.append((2 * (pair & 7) + jnp.where(value >= entry, 1, 0)).astype(jnp.float32))
        for column, top, low in zip(columns, tops, lows):
            top_ref[:, column] = jnp.concatenate(top, axis=0).astype(jnp.bfloat16)
            low_ref[:, column] = jnp.concatenate(low, axis=0).astype(jnp.bfloat16)
        return carry

    lax.fori_loop(0, rows // (width * LANES), chunk, 0)


def find_slots(turn, edge_codes, values):
    slots = jax.ShapeDtypeStruct((FEATS, values.shape[1]), jnp.bfloat16)
    return pl.pallas_call(
        lambda *refs: slot_kernel(turn, *refs),
        in_specs=in_vmem(2),
        out_specs=in_vmem(2),
        out_shape=[slots, slots],
        compiler_params=pltpu.CompilerParams(vmem_limit_bytes=16 << 20),
        cost_estimate=pl.CostEstimate(flops=10**7, bytes_accessed=10**7, transcendentals=0),
        name="slots",
    )(edge_codes, values)


def hist_kernel(hess_ref, top_ref, low_ref, mass_ref, high_ref, rest_ref, sum_ref, a0, b0):
    rows = top_ref.shape[1]
    shape = (FEATS, LANES)
    lane = lane_iota(shape)
    feat = lax.broadcasted_iota(jnp.int32, shape, 0)
    zero = jnp.zeros(shape, jnp.bfloat16)
    one = jnp.ones(shape, jnp.bfloat16)
    scaled = hess_ref[...] * 65536.0
    high = jnp.floor(scaled * (1.0 / 256.0))
    rest = scaled - high * 256.0
    wide = hess_ref.shape[1]
    for part in range(rows // wide):
        own = slice(part * wide, (part + 1) * wide)
        high_ref[:, own] = jnp.broadcast_to(high[part : part + 1], (FEATS, wide)).astype(jnp.bfloat16)
        rest_ref[:, own] = jnp.broadcast_to(rest[part : part + 1], (FEATS, wide)).astype(jnp.bfloat16)

    def make(step, a_ref, b_ref):
        for off in range(0, SPAN, LANES):
            at = pl.ds(pl.multiple_of(step * SPAN + off, LANES), LANES)
            own = slice(off, off + LANES)
            top, low, w_high, w_rest = top_ref[:, at], low_ref[:, at], high_ref[:, at], rest_ref[:, at]
            for k in range(16):
                hit = top == k
                a_ref[k * FEATS : (k + 1) * FEATS, own] = jnp.where(hit, w_high, zero)
                a_ref[(16 + k) * FEATS : (17 + k) * FEATS, own] = jnp.where(hit, w_rest, zero)
                b_ref[k * FEATS : (k + 1) * FEATS, own] = jnp.where(low <= k, one, zero)

    def add(a_ref, b_ref):
        sum_ref[...] += lax.dot_general(
            a_ref[...], b_ref[...], (((1,), (1,)), ((), ())), preferred_element_type=jnp.float32
        )

    sum_ref[...] = jnp.zeros_like(sum_ref)

    def step(index, carry):
        make(index, a0, b0)
        add(a0, b0)
        return carry

    lax.fori_loop(0, rows // SPAN, step, 0)

    for parity in range(2):
        point = 2 * lane + parity - 1
        column = (point & 7) * FEATS + feat
        result = jnp.zeros(shape, jnp.float32)
        before = jnp.zeros(shape, jnp.float32)
        for k in range(16):
            large = sum_ref[k * FEATS : (k + 1) * FEATS]
            small = sum_ref[(16 + k) * FEATS : (17 + k) * FEATS]
            block = (large * 256.0 + small) * (1.0 / 65536.0)
            here = jnp.where((point & 15) < 8, lane_take(block[:, :LANES], column), lane_take(block[:, LANES:], column))
            result = jnp.where((point >> 4) == k, before + here, result)
            before = before + lane_take(block[:, LANES:], 7 * FEATS + feat)
        mass_ref[:, parity * LANES : (parity + 1) * LANES] = result


def find_mass(hess, top, low):
    rows = top.shape[1]
    return pl.pallas_call(
        hist_kernel,
        in_specs=in_vmem(3),
        out_specs=in_vmem(1)[0],
        out_shape=jax.ShapeDtypeStruct((FEATS, 256), jnp.float32),
        scratch_shapes=[pltpu.VMEM((FEATS, rows), jnp.bfloat16)] * 2
        + [pltpu.VMEM((512, 256), jnp.float32)]
        + [pltpu.VMEM((512, SPAN), jnp.bfloat16), pltpu.VMEM((256, SPAN), jnp.bfloat16)],
        compiler_params=pltpu.CompilerParams(vmem_limit_bytes=24 << 20),
        cost_estimate=pl.CostEstimate(flops=4 * 10**9, bytes_accessed=10**7, transcendentals=0),
        name="hist",
    )(hess, top, low)


def cuts_kernel(codes_ref, ranks_ref, first_ref, second_ref, cuts_ref):
    shape = (FEATS, LANES)
    lane = lane_iota(shape)
    group = lax.axis_index("rows") // 8
    at = pl.ds(pl.multiple_of(group * FEATS, FEATS), FEATS)
    edge_even, edge_odd = even_odd(codes_ref[at, :])
    edge_next = lane_take(edge_even, (lane + 1) & (LANES - 1))
    mass = first_ref[...] + second_ref[...]
    mass_even, mass_odd = mass[:, :LANES], mass[:, LANES:]
    mass_next = lane_take(mass_even, (lane + 1) & (LANES - 1))
    total = jnp.broadcast_to(mass_odd[:, LANES - 1 :], shape)
    ranks = ranks_ref[at, :].astype(jnp.float32)
    orders = [jnp.where(lane == 0, 255, 2 * lane - 1), 2 * lane]
    targets = [pick_columns(ranks, order) * (1.0 / 65792.0) * total for order in orders]
    pairs = search_pairs([(mass_even, spread(mass_even))] * 2, targets)
    for side, (target, pair) in enumerate(zip(targets, pairs)):
        mid_mass = lane_take(mass_odd, pair)
        mid_edge = lane_take(edge_odd, pair)
        above = target >= mid_mass
        low_mass = jnp.where(above, mid_mass, lane_take(mass_even, pair))
        high_mass = jnp.where(above, lane_take(mass_next, pair), mid_mass)
        low_edge = jnp.where(above, mid_edge, lane_take(edge_even, pair))
        high_edge = jnp.where(above, lane_take(edge_next, pair), mid_edge)
        part = (target - low_mass) / (high_mass - low_mass)
        cuts_ref[:, side * LANES : (side + 1) * LANES] = low_edge + part * (high_edge - low_edge)


def find_cuts(edge_codes, cut_ranks, first, second):
    return pl.pallas_call(
        cuts_kernel,
        in_specs=in_vmem(4),
        out_specs=in_vmem(1)[0],
        out_shape=jax.ShapeDtypeStruct((FEATS, 256), jnp.float32),
        name="cuts",
    )(edge_codes, cut_ranks, first, second)


def place_group(raw, odd, values, write):
    shape = odd.shape
    lane = lane_iota(shape)
    last = jnp.broadcast_to(raw[:, :1], shape)
    even = jnp.where(lane == 0, -16.0, raw)
    after = jnp.where(lane == LANES - 1, last, lane_take(even, (lane + 1) & (LANES - 1)))
    inv_low = 1.0 / (odd - even)
    inv_high = 1.0 / (after - odd)
    inv_last = 1.0 / (16.0 - last)
    table = (even, spread(even))
    pairs = search_pairs([table] * len(values), values)
    knots = [lane_take(odd, pair) for pair in pairs]
    highs = [lane_take(inv_high, pair) for pair in pairs]
    lows = [lane_take(inv_low, pair) for pair in pairs]
    for index, (value, pair, knot, high, low) in enumerate(zip(values, pairs, knots, highs, lows)):
        inside = (2 * pair + 1).astype(jnp.float32) + (value - knot) * jnp.where(value >= knot, high, low)
        write(index, jnp.where(value >= last, 256.0 + (value - last) * inv_last, inside))


def place_kernel(c0, c1, c2, c3, values_ref, out_ref, cuts_ref):
    blocks, feats, wide = out_ref.shape
    mine = lax.axis_index("rows") // 8
    for turn, c_ref in enumerate((c0, c1, c2, c3)):
        group = (mine + 4 - turn) % 4
        cuts_ref[pl.ds(pl.multiple_of(group * FEATS, FEATS), FEATS), :] = c_ref[...]

    def step(index, carry):
        at = pl.ds(pl.multiple_of(index * 8, 8), 8)
        values = [values_ref[at, part * LANES : (part + 1) * LANES] for part in range(blocks * wide // LANES)]

        def write(part, value):
            lanes = part * LANES % wide
            out_ref[part * LANES // wide, at, lanes : lanes + LANES] = value

        place_group(cuts_ref[at, :LANES], cuts_ref[at, LANES:], values, write)
        return carry

    lax.fori_loop(0, feats // 8, step, 0)


def place(cuts, values):
    feats, rows = values.shape
    return pl.pallas_call(
        place_kernel,
        in_specs=in_vmem(5),
        out_specs=in_vmem(1)[0],
        out_shape=jax.ShapeDtypeStruct((8, feats, rows // 8), jnp.float32),
        scratch_shapes=[pltpu.VMEM((feats, 256), jnp.float32)],
        compiler_params=pltpu.CompilerParams(vmem_limit_bytes=16 << 20),
        name="place",
    )(*cuts, values)


def flip_rows(array, flip):
    return lax.ppermute(array, "rows", [(i, i ^ flip) for i in range(32)])


def turn_rows(array, turn):
    return lax.ppermute(array, "rows", [(i, (i + 8 * turn) % 32) for i in range(32)])


def on_device(feature_values, hessian_codes, edge_codes, cut_ranks):
    hess_own = hessian_codes.astype(jnp.float32) * (1.0 / 65536.0)
    hess = lax.all_gather(hess_own, "feat", axis=0)
    slots = [find_slots(turn, edge_codes, feature_values) for turn in range(4)]
    parts = [turn_rows(find_mass(hess, *slots[turn]), turn) for turn in (1, 2, 3)]
    mass = find_mass(hess, *slots[0]) + parts[0] + parts[1] + parts[2]
    for flip in (1, 2):
        mass = mass + flip_rows(mass, flip)
    cuts = find_cuts(edge_codes, cut_ranks, mass, flip_rows(mass, 4))
    cuts = [cuts] + [turn_rows(cuts, turn) for turn in (1, 2, 3)]
    positions = place(cuts, feature_values)
    return lax.all_to_all(positions, "feat", split_axis=0, concat_axis=0, tiled=True).reshape(512, -1)


def solution(mesh):
    placed = (P("feat", "rows"), P(("rows", "feat")), P("feat", None), P("feat", None))
    return jax.shard_map(
        on_device, mesh=mesh, in_specs=placed, out_specs=P(None, ("rows", "feat")), check_vma=False
    )
```

```python
import jax
import jax.numpy as jnp
from jax import lax
from jax.experimental import pallas as pl
from jax.experimental.pallas import tpu as pltpu
from jax.sharding import PartitionSpec as P

LANES = 128
FEATS = 16
DEPTH = 4
SPAN = 2048


def in_vmem(count):
    return [pl.BlockSpec(memory_space=pltpu.VMEM)] * count


def lane_take(table, index):
    return jnp.take_along_axis(table, index, axis=1, mode="promise_in_bounds")


def pick_columns(wide, index):
    low = lane_take(wide[:, :LANES], index & (LANES - 1))
    high = lane_take(wide[:, LANES:], index & (LANES - 1))
    return jnp.where(index < LANES, low, high)


def lane_iota(shape):
    return lax.broadcasted_iota(jnp.int32, shape, 1)


def choose(marks, low, high, masks):
    middle = (low + high) // 2
    if not masks:
        return marks[middle]
    upper = choose(marks, middle, high, masks[1:])
    return jnp.where(masks[0], upper, choose(marks, low, middle, masks[1:]))


def spread(even):
    return {i: jnp.broadcast_to(even[:, i : i + 1], even.shape) for i in range(128 >> DEPTH, 128, 128 >> DEPTH)}


def search_pairs(tables, values):
    masks = [[] for _ in values]
    for _ in range(DEPTH):
        for (_, marks), mask, value in zip(tables, masks, values):
            mask.append(value >= choose(marks, 0, LANES, mask))
    bases = []
    for mask in masks:
        base = jnp.where(mask[0], 64, 0)
        for level in range(1, DEPTH):
            base = base + jnp.where(mask[level], 64 >> level, 0)
        bases.append(base)
    step = 64 >> DEPTH
    while step:
        probes = [base + step for base in bases]
        entries = [lane_take(even, probe) for (even, _), probe in zip(tables, probes)]
        bases = [jnp.where(v >= e, p, b) for v, e, p, b in zip(values, entries, probes, bases)]
        step //= 2
    return bases


def even_odd(codes):
    lane = lane_iota((codes.shape[0], LANES))
    edges = codes.astype(jnp.float32) * (1.0 / 256.0)
    return pick_columns(edges, 2 * lane), pick_columns(edges, 2 * lane + 1)


def slot_kernel(turn, codes_ref, values_ref, top_ref, low_ref):
    rows = values_ref.shape[1]
    width = 32
    group = (lax.axis_index("rows") // 8 + turn) % 4
    tables = []
    for half in range(2):
        at = pl.ds(pl.multiple_of(group * FEATS + 8 * half, 8), 8)
        even, odd = even_odd(codes_ref[at, :])
        tables.append((at, odd, (even, spread(even))))

    def chunk(step, carry):
        columns = [pl.ds(pl.multiple_of((step * width + part) * LANES, LANES), LANES) for part in range(width)]
        tops, lows = [[] for _ in columns], [[] for _ in columns]
        for at, odd, table in tables:
            values = [values_ref[at, column] for column in columns]
            pairs = search_pairs([table] * width, values)
            entries = [lane_take(odd, pair) for pair in pairs]
            for top, low, value, pair, entry in zip(tops, lows, values, pairs, entries):
                top.append((pair >> 3).astype(jnp.float32))
                low.append((2 * (pair & 7) + jnp.where(value >= entry, 1, 0)).astype(jnp.float32))
        for column, top, low in zip(columns, tops, lows):
            top_ref[:, column] = jnp.concatenate(top, axis=0).astype(jnp.bfloat16)
            low_ref[:, column] = jnp.concatenate(low, axis=0).astype(jnp.bfloat16)
        return carry

    lax.fori_loop(0, rows // (width * LANES), chunk, 0)


def find_slots(turn, edge_codes, values):
    slots = jax.ShapeDtypeStruct((FEATS, values.shape[1]), jnp.bfloat16)
    return pl.pallas_call(
        lambda *refs: slot_kernel(turn, *refs),
        in_specs=in_vmem(2),
        out_specs=in_vmem(2),
        out_shape=[slots, slots],
        compiler_params=pltpu.CompilerParams(vmem_limit_bytes=16 << 20),
        cost_estimate=pl.CostEstimate(flops=10**7, bytes_accessed=10**7, transcendentals=0),
        name="slots",
    )(edge_codes, values)


def hist_kernel(hess_ref, top_ref, low_ref, mass_ref, high_ref, rest_ref, sum_ref, a0, b0):
    rows = top_ref.shape[1]
    shape = (FEATS, LANES)
    lane = lane_iota(shape)
    feat = lax.broadcasted_iota(jnp.int32, shape, 0)
    zero = jnp.zeros(shape, jnp.bfloat16)
    one = jnp.ones(shape, jnp.bfloat16)
    scaled = hess_ref[...] * 65536.0
    high = jnp.floor(scaled * (1.0 / 256.0))
    rest = scaled - high * 256.0
    wide = hess_ref.shape[1]
    me = lax.axis_index("feat")
    for part in range(rows // wide):
        own = pl.ds(pl.multiple_of((part ^ me) * wide, wide), wide)
        high_ref[:, own] = jnp.broadcast_to(high[part : part + 1], (FEATS, wide)).astype(jnp.bfloat16)
        rest_ref[:, own] = jnp.broadcast_to(rest[part : part + 1], (FEATS, wide)).astype(jnp.bfloat16)

    def make(step, a_ref, b_ref):
        for off in range(0, SPAN, LANES):
            at = pl.ds(pl.multiple_of(step * SPAN + off, LANES), LANES)
            own = slice(off, off + LANES)
            top, low, w_high, w_rest = top_ref[:, at], low_ref[:, at], high_ref[:, at], rest_ref[:, at]
            for k in range(16):
                hit = top == k
                a_ref[k * FEATS : (k + 1) * FEATS, own] = jnp.where(hit, w_high, zero)
                a_ref[(16 + k) * FEATS : (17 + k) * FEATS, own] = jnp.where(hit, w_rest, zero)
                b_ref[k * FEATS : (k + 1) * FEATS, own] = jnp.where(low <= k, one, zero)

    def add(a_ref, b_ref):
        sum_ref[...] += lax.dot_general(
            a_ref[...], b_ref[...], (((1,), (1,)), ((), ())), preferred_element_type=jnp.float32
        )

    sum_ref[...] = jnp.zeros_like(sum_ref)

    def step(index, carry):
        make(index, a0, b0)
        add(a0, b0)
        return carry

    lax.fori_loop(0, rows // SPAN, step, 0)

    points = [2 * lane - 1, 2 * lane]
    columns = [(point & 7) * FEATS + feat for point in points]
    results = [jnp.zeros(shape, jnp.float32)] * 2
    before = jnp.zeros(shape, jnp.float32)
    for k in range(16):
        large = sum_ref[k * FEATS : (k + 1) * FEATS]
        small = sum_ref[(16 + k) * FEATS : (17 + k) * FEATS]
        block = (large * 256.0 + small) * (1.0 / 65536.0)
        for parity, (point, column) in enumerate(zip(points, columns)):
            here = jnp.where((point & 15) < 8, lane_take(block[:, :LANES], column), lane_take(block[:, LANES:], column))
            results[parity] = jnp.where((point >> 4) == k, before + here, results[parity])
        before = before + lane_take(block[:, LANES:], 7 * FEATS + feat)
    mass_ref[:, :LANES] = results[0]
    mass_ref[:, LANES:] = results[1]


def find_mass(hess, top, low):
    rows = top.shape[1]
    return pl.pallas_call(
        hist_kernel,
        in_specs=in_vmem(3),
        out_specs=in_vmem(1)[0],
        out_shape=jax.ShapeDtypeStruct((FEATS, 256), jnp.float32),
        scratch_shapes=[pltpu.VMEM((FEATS, rows), jnp.bfloat16)] * 2
        + [pltpu.VMEM((512, 256), jnp.float32)]
        + [pltpu.VMEM((512, SPAN), jnp.bfloat16), pltpu.VMEM((256, SPAN), jnp.bfloat16)],
        compiler_params=pltpu.CompilerParams(vmem_limit_bytes=24 << 20),
        cost_estimate=pl.CostEstimate(flops=4 * 10**9, bytes_accessed=10**7, transcendentals=0),
        name="hist",
    )(hess, top, low)


def cuts_kernel(codes_ref, ranks_ref, first_ref, second_ref, cuts_ref):
    shape = (FEATS, LANES)
    lane = lane_iota(shape)
    group = lax.axis_index("rows") // 8
    at = pl.ds(pl.multiple_of(group * FEATS, FEATS), FEATS)
    edge_even, edge_odd = even_odd(codes_ref[at, :])
    edge_next = lane_take(edge_even, (lane + 1) & (LANES - 1))
    mass = first_ref[...] + second_ref[...]
    mass_even, mass_odd = mass[:, :LANES], mass[:, LANES:]
    mass_next = lane_take(mass_even, (lane + 1) & (LANES - 1))
    total = jnp.broadcast_to(mass_odd[:, LANES - 1 :], shape)
    ranks = ranks_ref[at, :].astype(jnp.float32)
    orders = [jnp.where(lane == 0, 255, 2 * lane - 1), 2 * lane]
    targets = [pick_columns(ranks, order) * (1.0 / 65792.0) * total for order in orders]
    pairs = search_pairs([(mass_even, spread(mass_even))] * 2, targets)
    for side, (target, pair) in enumerate(zip(targets, pairs)):
        mid_mass = lane_take(mass_odd, pair)
        mid_edge = lane_take(edge_odd, pair)
        above = target >= mid_mass
        low_mass = jnp.where(above, mid_mass, lane_take(mass_even, pair))
        high_mass = jnp.where(above, lane_take(mass_next, pair), mid_mass)
        low_edge = jnp.where(above, mid_edge, lane_take(edge_even, pair))
        high_edge = jnp.where(above, lane_take(edge_next, pair), mid_edge)
        part = (target - low_mass) / (high_mass - low_mass)
        cuts_ref[:, side * LANES : (side + 1) * LANES] = low_edge + part * (high_edge - low_edge)


def find_cuts(edge_codes, cut_ranks, first, second):
    return pl.pallas_call(
        cuts_kernel,
        in_specs=in_vmem(4),
        out_specs=in_vmem(1)[0],
        out_shape=jax.ShapeDtypeStruct((FEATS, 256), jnp.float32),
        compiler_params=pltpu.CompilerParams(vmem_limit_bytes=4 << 20),
        name="cuts",
    )(edge_codes, cut_ranks, first, second)


def place_group(raw, odd, values, write):
    shape = odd.shape
    lane = lane_iota(shape)
    last = jnp.broadcast_to(raw[:, :1], shape)
    even = jnp.where(lane == 0, -16.0, raw)
    after = jnp.where(lane == LANES - 1, last, lane_take(even, (lane + 1) & (LANES - 1)))
    inv_low = 1.0 / (odd - even)
    inv_high = 1.0 / (after - odd)
    inv_last = 1.0 / (16.0 - last)
    table = (even, spread(even))
    pairs = search_pairs([table] * len(values), values)
    knots = [lane_take(odd, pair) for pair in pairs]
    highs = [lane_take(inv_high, pair) for pair in pairs]
    lows = [lane_take(inv_low, pair) for pair in pairs]
    for index, (value, pair, knot, high, low) in enumerate(zip(values, pairs, knots, highs, lows)):
        inside = (2 * pair + 1).astype(jnp.float32) + (value - knot) * jnp.where(value >= knot, high, low)
        write(index, jnp.where(value >= last, 256.0 + (value - last) * inv_last, inside))


def first_kernel(moves, c0, c1, c2, c3, values_ref, cuts_ref, *out_refs):
    mine = lax.axis_index("rows") // 8
    for turn, c_ref in enumerate((c0, c1, c2, c3)):
        group = (mine + 4 - turn) % 4
        cuts_ref[pl.ds(pl.multiple_of(group * FEATS, FEATS), FEATS), :] = c_ref[...]
    place_kernel(moves, cuts_ref, values_ref, *out_refs)


def place_kernel(moves, cuts_ref, values_ref, *out_refs):
    feats, wide = out_refs[0].shape
    bases = [owner(move) * wide for move in moves]

    def step(index, carry):
        at = pl.ds(pl.multiple_of(index * 8, 8), 8)
        values, places = [], []
        for base, out_ref in zip(bases, out_refs):
            for part in range(0, wide, LANES):
                values.append(values_ref[at, pl.ds(pl.multiple_of(base + part, LANES), LANES)])
                places.append((out_ref, part))

        def write(part, value):
            out_ref, lanes = places[part]
            out_ref[at, lanes : lanes + LANES] = value

        place_group(cuts_ref[at, :LANES], cuts_ref[at, LANES:], values, write)
        return carry

    lax.fori_loop(0, feats // 8, step, 0)


def place(moves, cuts, values):
    feats, rows = values.shape
    block = jax.ShapeDtypeStruct((feats, rows // 8), jnp.float32)
    first = len(cuts) > 1
    kernel = first_kernel if first else place_kernel
    outs = [jax.ShapeDtypeStruct((feats, 256), jnp.float32)] * first + [block] * len(moves)
    return pl.pallas_call(
        lambda *refs: kernel(moves, *refs),
        in_specs=in_vmem(len(cuts) + 1),
        out_specs=in_vmem(len(outs)),
        out_shape=outs,
        compiler_params=pltpu.CompilerParams(vmem_limit_bytes=16 << 20),
        cost_estimate=pl.CostEstimate(flops=10**7 * len(moves), bytes_accessed=10**6, transcendentals=0),
        name="place",
    )(*cuts, values)


def join_kernel(moves, *refs):
    *parts, out_ref, sems = refs
    feats = parts[0].shape[0]
    copies = []
    for index, (move, part) in enumerate(zip(moves, parts)):
        back = (-move[0], move[1])
        rows = pl.ds(pl.multiple_of(owner(back) * feats, feats), feats)
        copies.append(pltpu.make_async_copy(part, out_ref.at[rows, :], sems.at[index]))
    for copy in copies:
        copy.start()
    for copy in copies:
        copy.wait()


def join(moves, parts):
    feats, wide = parts[0].shape
    return pl.pallas_call(
        lambda *refs: join_kernel(moves, *refs),
        in_specs=in_vmem(len(parts)),
        out_specs=pl.BlockSpec(memory_space=pl.ANY),
        out_shape=jax.ShapeDtypeStruct((len(parts) * feats, wide), jnp.float32),
        scratch_shapes=[pltpu.SemaphoreType.DMA((len(parts),))],
        compiler_params=pltpu.CompilerParams(vmem_limit_bytes=4 << 20),
        name="join",
    )(*parts)


def owner(move):
    me = lax.axis_index("feat")
    return (me // 2 + move[0] + 4) % 4 * 2 + (me % 2 ^ move[1])


def send_feat(array, move):
    return lax.ppermute(array, "feat", [(i, (i // 2 + move[0]) % 4 * 2 + (i % 2 ^ move[1])) for i in range(8)])


def flip_feat(array, flip):
    return lax.ppermute(array, "feat", [(i, i ^ flip) for i in range(8)])


def flip_rows(array, flip):
    return lax.ppermute(array, "rows", [(i, i ^ flip) for i in range(32)])


def turn_rows(array, turn):
    return lax.ppermute(array, "rows", [(i, (i + 8 * turn) % 32) for i in range(32)])


def on_device(feature_values, hessian_codes, edge_codes, cut_ranks):
    hess_own = hessian_codes.astype(jnp.float32) * (1.0 / 65536.0)
    hess = hess_own.reshape(1, -1)
    for flip in (1, 2, 4):
        hess = jnp.concatenate([hess, flip_feat(hess, flip)], axis=0)
    slots = [find_slots(turn, edge_codes, feature_values) for turn in range(4)]
    parts = [turn_rows(find_mass(hess, *slots[turn]), turn) for turn in (1, 2, 3)]
    mass = find_mass(hess, *slots[0]) + parts[0] + parts[1] + parts[2]
    for flip in (1, 2):
        mass = mass + flip_rows(mass, flip)
    cuts = find_cuts(edge_codes, cut_ranks, mass, flip_rows(mass, 4))
    cuts = [cuts] + [turn_rows(cuts, turn) for turn in (1, 2, 3)]
    stages = [[(2, 0), (2, 1)], [(1, 0), (3, 0)], [(1, 1), (3, 1)], [(0, 1), (0, 0)]]
    moves, parts = [], []
    for stage in stages:
        outs = place(stage, cuts, feature_values)
        if len(cuts) > 1:
            cuts, *outs = outs
            cuts = [cuts]
        moves += stage
        parts += [send_feat(out, move) if move != (0, 0) else out for out, move in zip(outs, stage)]
    return join(moves, parts)


def solution(mesh):
    placed = (P("feat", "rows"), P(("rows", "feat")), P("feat", None), P("feat", None))
    return jax.shard_map(
        on_device, mesh=mesh, in_specs=placed, out_specs=P(None, ("rows", "feat")), check_vma=False
    )
```

```python
import jax
import jax.numpy as jnp
from jax import lax
from jax.experimental import pallas as pl
from jax.experimental.pallas import tpu as pltpu
from jax.sharding import PartitionSpec as P

LANES = 128
FEATS = 16
DEPTH = 4
TILE = 256
UNROLL = 8


def in_vmem(count):
    return [pl.BlockSpec(memory_space=pltpu.VMEM)] * count


def lane_take(table, index):
    return jnp.take_along_axis(table, index, axis=1, mode="promise_in_bounds")


def pick_columns(wide, index):
    low = lane_take(wide[:, :LANES], index & (LANES - 1))
    high = lane_take(wide[:, LANES:], index & (LANES - 1))
    return jnp.where(index < LANES, low, high)


def lane_iota(shape):
    return lax.broadcasted_iota(jnp.int32, shape, 1)


def choose(marks, low, high, masks):
    middle = (low + high) // 2
    if not masks:
        return marks[middle]
    upper = choose(marks, middle, high, masks[1:])
    return jnp.where(masks[0], upper, choose(marks, low, middle, masks[1:]))


def spread(even):
    return {i: jnp.broadcast_to(even[:, i : i + 1], even.shape) for i in range(128 >> DEPTH, 128, 128 >> DEPTH)}


def search_pairs(tables, values):
    masks = [[] for _ in values]
    for _ in range(DEPTH):
        for (_, marks), mask, value in zip(tables, masks, values):
            mask.append(value >= choose(marks, 0, LANES, mask))
    bases = []
    for mask in masks:
        base = jnp.where(mask[0], 64, 0)
        for level in range(1, DEPTH):
            base = base + jnp.where(mask[level], 64 >> level, 0)
        bases.append(base)
    step = 64 >> DEPTH
    while step:
        probes = [base + step for base in bases]
        entries = [lane_take(even, probe) for (even, _), probe in zip(tables, probes)]
        bases = [jnp.where(v >= e, p, b) for v, e, p, b in zip(values, entries, probes, bases)]
        step //= 2
    return bases


def even_odd(codes):
    lane = lane_iota((codes.shape[0], LANES))
    edges = codes.astype(jnp.float32) * (1.0 / 256.0)
    return pick_columns(edges, 2 * lane), pick_columns(edges, 2 * lane + 1)


def slot_kernel(turn, codes_hbm, values_hbm, top_ref, low_ref, codes_ref, values_ref, sems):
    rows = values_ref.shape[1]
    width = 32
    group = (lax.axis_index("rows") // 8 + turn) % 4
    own = pl.ds(pl.multiple_of(group * FEATS, FEATS), FEATS)
    span = rows // 2
    copies = [pltpu.make_async_copy(codes_hbm.at[own, :], codes_ref, sems.at[2])]
    for part in range(2):
        at = slice(part * span, (part + 1) * span)
        copies.append(pltpu.make_async_copy(values_hbm.at[own, at], values_ref.at[:, at], sems.at[part]))
    for copy in copies:
        copy.start()
    copies[0].wait()
    tables = []
    for half in range(2):
        at = slice(8 * half, 8 * half + 8)
        even, odd = even_odd(codes_ref[at, :])
        tables.append((at, odd, (even, spread(even))))

    def chunk(step, carry):
        columns = [pl.ds(pl.multiple_of((step * width + part) * LANES, LANES), LANES) for part in range(width)]
        tops, lows = [[] for _ in columns], [[] for _ in columns]
        for at, odd, table in tables:
            values = [values_ref[at, column] for column in columns]
            pairs = search_pairs([table] * width, values)
            entries = [lane_take(odd, pair) for pair in pairs]
            for top, low, value, pair, entry in zip(tops, lows, values, pairs, entries):
                top.append((pair >> 3).astype(jnp.float32))
                low.append((2 * (pair & 7) + jnp.where(value >= entry, 1, 0)).astype(jnp.float32))
        for column, top, low in zip(columns, tops, lows):
            top_ref[:, column] = jnp.concatenate(top, axis=0).astype(jnp.bfloat16)
            low_ref[:, column] = jnp.concatenate(low, axis=0).astype(jnp.bfloat16)
        return carry

    steps = span // (width * LANES)
    for part in range(2):
        copies[1 + part].wait()
        lax.fori_loop(part * steps, (part + 1) * steps, chunk, 0)


def find_slots(turn, edge_codes, values):
    rows = values.shape[1]
    slots = jax.ShapeDtypeStruct((FEATS, rows), jnp.bfloat16)
    return pl.pallas_call(
        lambda *refs: slot_kernel(turn, *refs),
        in_specs=[pl.BlockSpec(memory_space=pltpu.HBM)] * 2,
        out_specs=in_vmem(2),
        out_shape=[slots, slots],
        scratch_shapes=[
            pltpu.VMEM((FEATS, 256), jnp.int32),
            pltpu.VMEM((FEATS, rows), jnp.float32),
            pltpu.SemaphoreType.DMA((3,)),
        ],
        compiler_params=pltpu.CompilerParams(vmem_limit_bytes=16 << 20),
        cost_estimate=pl.CostEstimate(flops=10**7, bytes_accessed=10**7, transcendentals=0),
        name="slots",
    )(
        pltpu.with_memory_space_constraint(edge_codes, pltpu.HBM),
        pltpu.with_memory_space_constraint(values, pltpu.HBM),
    )


def hist_kernel(hess_ref, top_ref, low_ref, mass_ref, high_ref, rest_ref, sum_ref):
    rows = top_ref.shape[1]
    shape = (FEATS, LANES)
    lane = lane_iota(shape)
    feat = lax.broadcasted_iota(jnp.int32, shape, 0)
    scaled = hess_ref[...] * 65536.0
    high = jnp.floor(scaled * (1.0 / 256.0))
    rest = scaled - high * 256.0
    wide = hess_ref.shape[1]
    me = lax.axis_index("feat")
    for part in range(rows // wide):
        own = pl.ds(pl.multiple_of((part ^ me) * wide, wide), wide)
        high_ref[:, own] = jnp.broadcast_to(high[part : part + 1], (FEATS, wide)).astype(jnp.bfloat16)
        rest_ref[:, own] = jnp.broadcast_to(rest[part : part + 1], (FEATS, wide)).astype(jnp.bfloat16)

    def multiply(*sums):
        zero = jnp.zeros((FEATS, TILE), jnp.bfloat16)
        one = jnp.ones((FEATS, TILE), jnp.bfloat16)
        units = (sums[:16], sums[16:])

        def step(index, carry):
            for turn in range(UNROLL):
                spots = [pl.ds(pl.multiple_of(((index * UNROLL + turn) * 2 + unit) * TILE, TILE), TILE) for unit in range(2)]
                for unit, at in enumerate(spots):
                    low = low_ref[:, at]
                    below = jnp.concatenate([jnp.where(low <= k, one, zero) for k in range(16)], axis=0)
                    pltpu.matmul_push_rhs(below, turn % 2, unit, transpose=True)
                for unit, at in enumerate(spots):
                    top, w_high, w_rest = top_ref[:, at], high_ref[:, at], rest_ref[:, at]
                    for k in range(16):
                        hit = top == k
                        weighted = jnp.concatenate([jnp.where(hit, w_high, zero), jnp.where(hit, w_rest, zero)], axis=0)
                        pltpu.matmul_acc_lhs(units[unit][k], weighted, load_staged_rhs=turn % 2 if k == 0 else None)
            return carry

        lax.fori_loop(0, rows // (2 * TILE * UNROLL), step, 0)
        for k in range(16):
            both = pltpu.matmul_pop(units[0][k]) + pltpu.matmul_pop(units[1][k])
            sum_ref[k * FEATS : (k + 1) * FEATS] = both[:FEATS] * (1.0 / 256.0) + both[FEATS:] * (1.0 / 65536.0)

    pl.run_scoped(multiply, *[pltpu.ACC(mxu_id=unit)((2 * FEATS, TILE), jnp.float32) for unit in range(2) for _ in range(16)])

    points = [2 * lane - 1, 2 * lane]
    columns = [(point & 7) * FEATS + feat for point in points]
    results = [jnp.zeros(shape, jnp.float32)] * 2
    before = jnp.zeros(shape, jnp.float32)
    for k in range(16):
        block = sum_ref[k * FEATS : (k + 1) * FEATS]
        for parity, (point, column) in enumerate(zip(points, columns)):
            here = jnp.where((point & 15) < 8, lane_take(block[:, :LANES], column), lane_take(block[:, LANES:], column))
            results[parity] = jnp.where((point >> 4) == k, before + here, results[parity])
        before = before + lane_take(block[:, LANES:], 7 * FEATS + feat)
    mass_ref[:, :LANES] = results[0]
    mass_ref[:, LANES:] = results[1]


def find_mass(hess, top, low):
    rows = top.shape[1]
    return pl.pallas_call(
        hist_kernel,
        in_specs=in_vmem(3),
        out_specs=in_vmem(1)[0],
        out_shape=jax.ShapeDtypeStruct((FEATS, 256), jnp.float32),
        scratch_shapes=[pltpu.VMEM((FEATS, rows), jnp.bfloat16)] * 2
        + [pltpu.VMEM((16 * FEATS, TILE), jnp.float32)],
        compiler_params=pltpu.CompilerParams(vmem_limit_bytes=24 << 20),
        cost_estimate=pl.CostEstimate(flops=4 * 10**9, bytes_accessed=10**7, transcendentals=0),
        name="hist",
    )(hess, top, low)


def cuts_kernel(codes_ref, ranks_ref, first_ref, second_ref, third_ref, cuts_ref):
    shape = (FEATS, LANES)
    lane = lane_iota(shape)
    group = lax.axis_index("rows") // 8
    at = pl.ds(pl.multiple_of(group * FEATS, FEATS), FEATS)
    edge_even, edge_odd = even_odd(codes_ref[at, :])
    edge_next = lane_take(edge_even, (lane + 1) & (LANES - 1))
    mass = first_ref[...] + second_ref[...] + third_ref[...]
    mass_even, mass_odd = mass[:, :LANES], mass[:, LANES:]
    mass_next = lane_take(mass_even, (lane + 1) & (LANES - 1))
    total = jnp.broadcast_to(mass_odd[:, LANES - 1 :], shape)
    ranks = ranks_ref[at, :].astype(jnp.float32)
    orders = [jnp.where(lane == 0, 255, 2 * lane - 1), 2 * lane]
    targets = [pick_columns(ranks, order) * (1.0 / 65792.0) * total for order in orders]
    pairs = search_pairs([(mass_even, spread(mass_even))] * 2, targets)
    for side, (target, pair) in enumerate(zip(targets, pairs)):
        mid_mass = lane_take(mass_odd, pair)
        mid_edge = lane_take(edge_odd, pair)
        above = target >= mid_mass
        low_mass = jnp.where(above, mid_mass, lane_take(mass_even, pair))
        high_mass = jnp.where(above, lane_take(mass_next, pair), mid_mass)
        low_edge = jnp.where(above, mid_edge, lane_take(edge_even, pair))
        high_edge = jnp.where(above, lane_take(edge_next, pair), mid_edge)
        part = (target - low_mass) / (high_mass - low_mass)
        cuts_ref[:, side * LANES : (side + 1) * LANES] = low_edge + part * (high_edge - low_edge)


def find_cuts(edge_codes, cut_ranks, *sums):
    return pl.pallas_call(
        cuts_kernel,
        in_specs=in_vmem(2 + len(sums)),
        out_specs=in_vmem(1)[0],
        out_shape=jax.ShapeDtypeStruct((FEATS, 256), jnp.float32),
        compiler_params=pltpu.CompilerParams(vmem_limit_bytes=4 << 20),
        name="cuts",
    )(edge_codes, cut_ranks, *sums)


def place_groups(groups):
    tables, all_values, rest = [], [], []
    for raw, odd, values, writes in groups:
        shape = odd.shape
        lane = lane_iota(shape)
        last = jnp.broadcast_to(raw[:, :1], shape)
        even = jnp.where(lane == 0, -16.0, raw)
        after = jnp.where(lane == LANES - 1, last, lane_take(even, (lane + 1) & (LANES - 1)))
        inv_low = 1.0 / (odd - even)
        inv_high = 1.0 / (after - odd)
        inv_last = 1.0 / (16.0 - last)
        tables += [(even, spread(even))] * len(values)
        all_values += values
        rest += [(odd, inv_low, inv_high, last, inv_last, write) for write in writes]
    pairs = search_pairs(tables, all_values)
    knots = [lane_take(item[0], pair) for item, pair in zip(rest, pairs)]
    lows = [lane_take(item[1], pair) for item, pair in zip(rest, pairs)]
    highs = [lane_take(item[2], pair) for item, pair in zip(rest, pairs)]
    for item, value, pair, knot, low, high in zip(rest, all_values, pairs, knots, lows, highs):
        last, inv_last, write = item[3:]
        inside = (2 * pair + 1).astype(jnp.float32) + (value - knot) * jnp.where(value >= knot, high, low)
        write(jnp.where(value >= last, 256.0 + (value - last) * inv_last, inside))


def first_kernel(moves, c0, c1, c2, c3, values_ref, cuts_ref, *out_refs):
    mine = lax.axis_index("rows") // 8
    for turn, c_ref in enumerate((c0, c1, c2, c3)):
        group = (mine + 4 - turn) % 4
        cuts_ref[pl.ds(pl.multiple_of(group * FEATS, FEATS), FEATS), :] = c_ref[...]
    place_kernel(moves, cuts_ref, values_ref, *out_refs)


def place_kernel(moves, cuts_ref, values_ref, *out_refs):
    feats, wide = out_refs[0].shape
    bases = [owner(move) * wide for move in moves]

    together = max(1, 8 // len(moves))

    def store(out_ref, at, part):
        def write(value):
            out_ref[at, part : part + LANES] = value

        return write

    def step(index, carry):
        groups = []
        for turn in range(together):
            at = pl.ds(pl.multiple_of((index * together + turn) * 8, 8), 8)
            values, writes = [], []
            for base, out_ref in zip(bases, out_refs):
                for part in range(0, wide, LANES):
                    values.append(values_ref[at, pl.ds(pl.multiple_of(base + part, LANES), LANES)])
                    writes.append(store(out_ref, at, part))
            groups.append((cuts_ref[at, :LANES], cuts_ref[at, LANES:], values, writes))
        place_groups(groups)
        return carry

    lax.fori_loop(0, feats // (8 * together), step, 0)


def place(moves, cuts, values):
    feats, rows = values.shape
    block = jax.ShapeDtypeStruct((feats, rows // 8), jnp.float32)
    first = len(cuts) > 1
    kernel = first_kernel if first else place_kernel
    outs = [jax.ShapeDtypeStruct((feats, 256), jnp.float32)] * first + [block] * len(moves)
    return pl.pallas_call(
        lambda *refs: kernel(moves, *refs),
        in_specs=in_vmem(len(cuts) + 1),
        out_specs=in_vmem(len(outs)),
        out_shape=outs,
        compiler_params=pltpu.CompilerParams(vmem_limit_bytes=16 << 20),
        cost_estimate=pl.CostEstimate(flops=10**7 * len(moves), bytes_accessed=10**6, transcendentals=0),
        name="place",
    )(*cuts, values)


def join_kernel(moves, *refs):
    *parts, out_ref, sems = refs
    feats = parts[0].shape[0]
    copies = []
    for index, (move, part) in enumerate(zip(moves, parts)):
        back = (-move[0], move[1])
        rows = pl.ds(pl.multiple_of(owner(back) * feats, feats), feats)
        copies.append(pltpu.make_async_copy(part, out_ref.at[rows, :], sems.at[index]))
    for copy in copies:
        copy.start()
    for copy in copies:
        copy.wait()


def join(moves, parts):
    feats, wide = parts[0].shape
    return pl.pallas_call(
        lambda *refs: join_kernel(moves, *refs),
        in_specs=in_vmem(len(parts)),
        out_specs=pl.BlockSpec(memory_space=pl.ANY),
        out_shape=jax.ShapeDtypeStruct((len(parts) * feats, wide), jnp.float32),
        scratch_shapes=[pltpu.SemaphoreType.DMA((len(parts),))],
        compiler_params=pltpu.CompilerParams(vmem_limit_bytes=4 << 20),
        name="join",
    )(*parts)


def owner(move):
    me = lax.axis_index("feat")
    return (me // 2 + move[0] + 4) % 4 * 2 + (me % 2 ^ move[1])


def send_feat(array, move):
    return lax.ppermute(array, "feat", [(i, (i // 2 + move[0]) % 4 * 2 + (i % 2 ^ move[1])) for i in range(8)])


def flip_feat(array, flip):
    return lax.ppermute(array, "feat", [(i, i ^ flip) for i in range(8)])


def shift_rows(array, shift):
    return lax.ppermute(array, "rows", [(i, i // 8 * 8 + (i + shift) % 8) for i in range(32)])


def turn_rows(array, turn):
    return lax.ppermute(array, "rows", [(i, (i + 8 * turn) % 32) for i in range(32)])


def on_device(feature_values, hessian_codes, edge_codes, cut_ranks):
    hess_own = hessian_codes.astype(jnp.float32) * (1.0 / 65536.0)
    hess = hess_own.reshape(1, -1)
    slots = {}
    codes = edge_codes
    for flip, turns in ((1, (1,)), (2, (2,)), (4, (3, 0))):
        other = flip_feat(hess, flip)
        for turn in turns:
            slots[turn] = find_slots(turn, codes, feature_values)
        hess = jnp.concatenate([hess, other], axis=0)
        if flip < 4:
            hess, slots[turn], codes = lax.optimization_barrier((hess, slots[turn], codes))
    parts = [turn_rows(find_mass(hess, *slots[turn]), turn) for turn in (1, 2, 3)]
    mass = find_mass(hess, *slots[0]) + parts[0] + parts[1] + parts[2]
    before = mass + shift_rows(mass, 1)
    around = before + shift_rows(mass, -1)
    cuts = find_cuts(edge_codes, cut_ranks, around, shift_rows(around, -3), shift_rows(before, 2))
    cuts = [cuts] + [turn_rows(cuts, turn) for turn in (1, 2, 3)]
    stages = [[(2, 0)], [(2, 1), (1, 0)], [(3, 0), (1, 1)], [(3, 1), (0, 1)], [(0, 0)]]
    moves, parts = [], []
    for stage in stages:
        outs = place(stage, cuts, feature_values)
        if len(cuts) > 1:
            cuts, *outs = outs
            cuts = [cuts]
        moves += stage
        parts += [send_feat(out, move) if move != (0, 0) else out for out, move in zip(outs, stage)]
    return join(moves, parts)


def solution(mesh):
    placed = (P("feat", "rows"), P(("rows", "feat")), P("feat", None), P("feat", None))
    return jax.shard_map(
        on_device, mesh=mesh, in_specs=placed, out_specs=P(None, ("rows", "feat")), check_vma=False
    )
```

```python
import jax
import jax.numpy as jnp
from jax import lax
from jax.experimental import pallas as pl
from jax.experimental.pallas import tpu as pltpu
from jax.sharding import PartitionSpec as P

LANES = 128
FEATS = 16
DEPTH = 4
TILE = 256
UNROLL = 8


def in_vmem(count):
    return [pl.BlockSpec(memory_space=pltpu.VMEM)] * count


def lane_take(table, index):
    return jnp.take_along_axis(table, index, axis=1, mode="promise_in_bounds")


def pick_columns(wide, index):
    low = lane_take(wide[:, :LANES], index & (LANES - 1))
    high = lane_take(wide[:, LANES:], index & (LANES - 1))
    return jnp.where(index < LANES, low, high)


def lane_iota(shape):
    return lax.broadcasted_iota(jnp.int32, shape, 1)


def choose(marks, low, high, masks):
    middle = (low + high) // 2
    if not masks:
        return marks[middle]
    upper = choose(marks, middle, high, masks[1:])
    return jnp.where(masks[0], upper, choose(marks, low, middle, masks[1:]))


def spread(even):
    return {i: jnp.broadcast_to(even[:, i : i + 1], even.shape) for i in range(128 >> DEPTH, 128, 128 >> DEPTH)}


def search_pairs(tables, values):
    masks = [[] for _ in values]
    for _ in range(DEPTH):
        for (_, marks), mask, value in zip(tables, masks, values):
            mask.append(value >= choose(marks, 0, LANES, mask))
    bases = []
    for mask in masks:
        base = jnp.where(mask[0], 64, 0)
        for level in range(1, DEPTH):
            base = base + jnp.where(mask[level], 64 >> level, 0)
        bases.append(base)
    step = 64 >> DEPTH
    while step:
        probes = [base + step for base in bases]
        entries = [lane_take(even, probe) for (even, _), probe in zip(tables, probes)]
        bases = [jnp.where(v >= e, p, b) for v, e, p, b in zip(values, entries, probes, bases)]
        step //= 2
    return bases


def even_odd(codes):
    lane = lane_iota((codes.shape[0], LANES))
    edges = codes.astype(jnp.float32) * (1.0 / 256.0)
    return pick_columns(edges, 2 * lane), pick_columns(edges, 2 * lane + 1)


def slot_kernel(turn, codes_hbm, values_hbm, top_ref, low_ref, codes_ref, values_ref, sems):
    rows = values_ref.shape[1]
    group = (lax.axis_index("rows") // 8 + turn) % 4
    own = pl.ds(pl.multiple_of(group * FEATS, FEATS), FEATS)
    span = rows // 2
    copies = [pltpu.make_async_copy(codes_hbm.at[own, :], codes_ref, sems.at[2])]
    for part in range(2):
        at = slice(part * span, (part + 1) * span)
        copies.append(pltpu.make_async_copy(values_hbm.at[own, at], values_ref.at[:, at], sems.at[part]))
    for copy in copies:
        copy.start()
    copies[0].wait()
    for part in range(2):
        copies[1 + part].wait()
        search_slots(0, codes_ref, values_ref, top_ref, low_ref, (part / 2, (part + 1) / 2))


def search_slots(first, codes_ref, values_ref, top_ref, low_ref, share):
    width = 32
    steps = values_ref.shape[1] // (width * LANES)
    tables = []
    for half in range(2):
        at = pl.ds(first + 8 * half, 8)
        even, odd = even_odd(codes_ref[at, :])
        tables.append((at, odd, (even, spread(even))))

    def chunk(step, carry):
        columns = [pl.ds(pl.multiple_of((step * width + part) * LANES, LANES), LANES) for part in range(width)]
        tops, lows = [[] for _ in columns], [[] for _ in columns]
        for at, odd, table in tables:
            values = [values_ref[at, column] for column in columns]
            pairs = search_pairs([table] * width, values)
            entries = [lane_take(odd, pair) for pair in pairs]
            for top, low, value, pair, entry in zip(tops, lows, values, pairs, entries):
                top.append((pair >> 3).astype(jnp.float32))
                low.append((2 * (pair & 7) + jnp.where(value >= entry, 1, 0)).astype(jnp.float32))
        for column, top, low in zip(columns, tops, lows):
            top_ref[:, column] = jnp.concatenate(top, axis=0).astype(jnp.bfloat16)
            low_ref[:, column] = jnp.concatenate(low, axis=0).astype(jnp.bfloat16)
        return carry

    lax.fori_loop(int(share[0] * steps), int(share[1] * steps), chunk, 0)


def near_slot_kernel(turn, codes_ref, values_ref, top_ref, low_ref):
    group = (lax.axis_index("rows") // 8 + turn) % 4
    search_slots(pl.multiple_of(group * FEATS, FEATS), codes_ref, values_ref, top_ref, low_ref, (0, 1))


def find_near_slots(turn, edge_codes, values):
    slots = jax.ShapeDtypeStruct((FEATS, values.shape[1]), jnp.bfloat16)
    return pl.pallas_call(
        lambda *refs: near_slot_kernel(turn, *refs),
        in_specs=in_vmem(2),
        out_specs=in_vmem(2),
        out_shape=[slots, slots],
        compiler_params=pltpu.CompilerParams(vmem_limit_bytes=16 << 20),
        cost_estimate=pl.CostEstimate(flops=10**7, bytes_accessed=10**7, transcendentals=0),
        name="slots",
    )(edge_codes, values)


def find_slots(turn, edge_codes, values):
    rows = values.shape[1]
    slots = jax.ShapeDtypeStruct((FEATS, rows), jnp.bfloat16)
    return pl.pallas_call(
        lambda *refs: slot_kernel(turn, *refs),
        in_specs=[pl.BlockSpec(memory_space=pltpu.HBM)] * 2,
        out_specs=in_vmem(2),
        out_shape=[slots, slots],
        scratch_shapes=[
            pltpu.VMEM((FEATS, 256), jnp.int32),
            pltpu.VMEM((FEATS, rows), jnp.float32),
            pltpu.SemaphoreType.DMA((3,)),
        ],
        compiler_params=pltpu.CompilerParams(vmem_limit_bytes=16 << 20),
        cost_estimate=pl.CostEstimate(flops=10**7, bytes_accessed=10**7, transcendentals=0),
        name="slots",
    )(
        pltpu.with_memory_space_constraint(edge_codes, pltpu.HBM),
        pltpu.with_memory_space_constraint(values, pltpu.HBM),
    )


def hist_kernel(hess_ref, top_ref, low_ref, mass_ref, high_ref, rest_ref, sum_ref):
    rows = top_ref.shape[1]
    shape = (FEATS, LANES)
    lane = lane_iota(shape)
    feat = lax.broadcasted_iota(jnp.int32, shape, 0)
    scaled = hess_ref[...] * 65536.0
    high = jnp.floor(scaled * (1.0 / 256.0))
    rest = scaled - high * 256.0
    wide = hess_ref.shape[1]
    me = lax.axis_index("feat")
    for part in range(rows // wide):
        own = pl.ds(pl.multiple_of((part ^ me) * wide, wide), wide)
        high_ref[:, own] = jnp.broadcast_to(high[part : part + 1], (FEATS, wide)).astype(jnp.bfloat16)
        rest_ref[:, own] = jnp.broadcast_to(rest[part : part + 1], (FEATS, wide)).astype(jnp.bfloat16)

    def multiply(*sums):
        zero = jnp.zeros((FEATS, TILE), jnp.bfloat16)
        one = jnp.ones((FEATS, TILE), jnp.bfloat16)
        units = (sums[:16], sums[16:])

        def step(index, carry):
            for turn in range(UNROLL):
                spots = [pl.ds(pl.multiple_of(((index * UNROLL + turn) * 2 + unit) * TILE, TILE), TILE) for unit in range(2)]
                for unit, at in enumerate(spots):
                    low = low_ref[:, at]
                    below = jnp.concatenate([jnp.where(low <= k, one, zero) for k in range(16)], axis=0)
                    pltpu.matmul_push_rhs(below, turn % 2, unit, transpose=True)
                for unit, at in enumerate(spots):
                    top, w_high, w_rest = top_ref[:, at], high_ref[:, at], rest_ref[:, at]
                    for k in range(16):
                        hit = top == k
                        weighted = jnp.concatenate([jnp.where(hit, w_high, zero), jnp.where(hit, w_rest, zero)], axis=0)
                        pltpu.matmul_acc_lhs(units[unit][k], weighted, load_staged_rhs=turn % 2 if k == 0 else None)
            return carry

        lax.fori_loop(0, rows // (2 * TILE * UNROLL), step, 0)
        for k in range(16):
            both = pltpu.matmul_pop(units[0][k]) + pltpu.matmul_pop(units[1][k])
            sum_ref[k * FEATS : (k + 1) * FEATS] = both[:FEATS] * (1.0 / 256.0) + both[FEATS:] * (1.0 / 65536.0)

    pl.run_scoped(multiply, *[pltpu.ACC(mxu_id=unit)((2 * FEATS, TILE), jnp.float32) for unit in range(2) for _ in range(16)])

    points = [2 * lane - 1, 2 * lane]
    columns = [(point & 7) * FEATS + feat for point in points]
    results = [jnp.zeros(shape, jnp.float32)] * 2
    before = jnp.zeros(shape, jnp.float32)
    for k in range(16):
        block = sum_ref[k * FEATS : (k + 1) * FEATS]
        for parity, (point, column) in enumerate(zip(points, columns)):
            here = jnp.where((point & 15) < 8, lane_take(block[:, :LANES], column), lane_take(block[:, LANES:], column))
            results[parity] = jnp.where((point >> 4) == k, before + here, results[parity])
        before = before + lane_take(block[:, LANES:], 7 * FEATS + feat)
    mass_ref[:, :LANES] = results[0]
    mass_ref[:, LANES:] = results[1]


def find_mass(hess, top, low):
    rows = top.shape[1]
    return pl.pallas_call(
        hist_kernel,
        in_specs=in_vmem(3),
        out_specs=in_vmem(1)[0],
        out_shape=jax.ShapeDtypeStruct((FEATS, 256), jnp.float32),
        scratch_shapes=[pltpu.VMEM((FEATS, rows), jnp.bfloat16)] * 2
        + [pltpu.VMEM((16 * FEATS, TILE), jnp.float32)],
        compiler_params=pltpu.CompilerParams(vmem_limit_bytes=24 << 20),
        cost_estimate=pl.CostEstimate(flops=4 * 10**9, bytes_accessed=10**7, transcendentals=0),
        name="hist",
    )(hess, top, low)


def cuts_kernel(codes_ref, ranks_ref, first_ref, second_ref, third_ref, cuts_ref):
    shape = (FEATS, LANES)
    lane = lane_iota(shape)
    group = lax.axis_index("rows") // 8
    at = pl.ds(pl.multiple_of(group * FEATS, FEATS), FEATS)
    edge_even, edge_odd = even_odd(codes_ref[at, :])
    edge_next = lane_take(edge_even, (lane + 1) & (LANES - 1))
    mass = first_ref[...] + second_ref[...] + third_ref[...]
    mass_even, mass_odd = mass[:, :LANES], mass[:, LANES:]
    mass_next = lane_take(mass_even, (lane + 1) & (LANES - 1))
    total = jnp.broadcast_to(mass_odd[:, LANES - 1 :], shape)
    ranks = ranks_ref[at, :].astype(jnp.float32)
    orders = [jnp.where(lane == 0, 255, 2 * lane - 1), 2 * lane]
    targets = [pick_columns(ranks, order) * (1.0 / 65792.0) * total for order in orders]
    pairs = search_pairs([(mass_even, spread(mass_even))] * 2, targets)
    for side, (target, pair) in enumerate(zip(targets, pairs)):
        mid_mass = lane_take(mass_odd, pair)
        mid_edge = lane_take(edge_odd, pair)
        above = target >= mid_mass
        low_mass = jnp.where(above, mid_mass, lane_take(mass_even, pair))
        high_mass = jnp.where(above, lane_take(mass_next, pair), mid_mass)
        low_edge = jnp.where(above, mid_edge, lane_take(edge_even, pair))
        high_edge = jnp.where(above, lane_take(edge_next, pair), mid_edge)
        part = (target - low_mass) / (high_mass - low_mass)
        cuts_ref[:, side * LANES : (side + 1) * LANES] = low_edge + part * (high_edge - low_edge)


def find_cuts(edge_codes, cut_ranks, *sums):
    return pl.pallas_call(
        cuts_kernel,
        in_specs=in_vmem(2 + len(sums)),
        out_specs=in_vmem(1)[0],
        out_shape=jax.ShapeDtypeStruct((FEATS, 256), jnp.float32),
        compiler_params=pltpu.CompilerParams(vmem_limit_bytes=4 << 20),
        name="cuts",
    )(edge_codes, cut_ranks, *sums)


def place_groups(groups):
    tables, all_values, rest = [], [], []
    for raw, odd, values, writes in groups:
        shape = odd.shape
        lane = lane_iota(shape)
        last = jnp.broadcast_to(raw[:, :1], shape)
        even = jnp.where(lane == 0, -16.0, raw)
        after = jnp.where(lane == LANES - 1, last, lane_take(even, (lane + 1) & (LANES - 1)))
        inv_low = 1.0 / (odd - even)
        inv_high = 1.0 / (after - odd)
        inv_last = 1.0 / (16.0 - last)
        tables += [(even, spread(even))] * len(values)
        all_values += values
        rest += [(odd, inv_low, inv_high, last, inv_last, write) for write in writes]
    pairs = search_pairs(tables, all_values)
    knots = [lane_take(item[0], pair) for item, pair in zip(rest, pairs)]
    lows = [lane_take(item[1], pair) for item, pair in zip(rest, pairs)]
    highs = [lane_take(item[2], pair) for item, pair in zip(rest, pairs)]
    for item, value, pair, knot, low, high in zip(rest, all_values, pairs, knots, lows, highs):
        last, inv_last, write = item[3:]
        inside = (2 * pair + 1).astype(jnp.float32) + (value - knot) * jnp.where(value >= knot, high, low)
        write(jnp.where(value >= last, 256.0 + (value - last) * inv_last, inside))


def collect_kernel(c0, c1, c2, c3, cuts_ref):
    mine = lax.axis_index("rows") // 8
    for turn, c_ref in enumerate((c0, c1, c2, c3)):
        group = (mine + 4 - turn) % 4
        cuts_ref[pl.ds(pl.multiple_of(group * FEATS, FEATS), FEATS), :] = c_ref[...]


def collect(parts):
    return pl.pallas_call(
        collect_kernel,
        in_specs=in_vmem(4),
        out_specs=in_vmem(1)[0],
        out_shape=jax.ShapeDtypeStruct((4 * FEATS, 256), jnp.float32),
        compiler_params=pltpu.CompilerParams(vmem_limit_bytes=4 << 20),
        name="collect",
    )(*parts)


def place_kernel(moves, cuts_ref, values_ref, *out_refs):
    wide = out_refs[0].shape[1]
    place_blocks([owner(move) * wide for move in moves], cuts_ref, values_ref, out_refs)


def place_blocks(bases, cuts_ref, values_ref, out_refs):
    feats, wide = out_refs[0].shape
    together = 4

    def store(out_ref, at, part):
        def write(value):
            out_ref[at, part : part + LANES] = value

        return write

    def step(index, carry):
        groups = []
        for turn in range(together):
            at = pl.ds(pl.multiple_of((index * together + turn) * 8, 8), 8)
            values, writes = [], []
            for base, out_ref in zip(bases, out_refs):
                for part in range(0, wide, LANES):
                    values.append(values_ref[at, pl.ds(pl.multiple_of(base + part, LANES), LANES)])
                    writes.append(store(out_ref, at, part))
            groups.append((cuts_ref[at, :LANES], cuts_ref[at, LANES:], values, writes))
        place_groups(groups)
        return carry

    lax.fori_loop(0, feats // (8 * together), step, 0)


def place(moves, cuts, values):
    feats, rows = values.shape
    block = jax.ShapeDtypeStruct((feats, rows // 8), jnp.float32)
    return pl.pallas_call(
        lambda *refs: place_kernel(moves, *refs),
        in_specs=in_vmem(2),
        out_specs=in_vmem(len(moves)),
        out_shape=[block] * len(moves),
        compiler_params=pltpu.CompilerParams(vmem_limit_bytes=16 << 20),
        cost_estimate=pl.CostEstimate(flops=10**7 * len(moves), bytes_accessed=10**6, transcendentals=0),
        name="place",
    )(cuts, values)


def cut_kernel(moves, values_hbm, *refs):
    *outs, sems = refs
    wide = outs[0].shape[1]
    copies = []
    for index, (move, out) in enumerate(zip(moves, outs)):
        at = pl.ds(pl.multiple_of(owner(move) * wide, wide), wide)
        copies.append(pltpu.make_async_copy(values_hbm.at[:, at], out, sems.at[index]))
    for copy in copies:
        copy.start()
    for copy in copies:
        copy.wait()


def cut_blocks(moves, values):
    feats, rows = values.shape
    return pl.pallas_call(
        lambda *refs: cut_kernel(moves, *refs),
        in_specs=[pl.BlockSpec(memory_space=pltpu.HBM)],
        out_specs=in_vmem(len(moves)),
        out_shape=[jax.ShapeDtypeStruct((feats, rows // 8), jnp.float32)] * len(moves),
        scratch_shapes=[pltpu.SemaphoreType.DMA((len(moves),))],
        compiler_params=pltpu.CompilerParams(vmem_limit_bytes=4 << 20),
        name="cut",
    )(pltpu.with_memory_space_constraint(values, pltpu.HBM))


def finish_kernel(moves, far_moves, *refs):
    count, far = len(moves), len(far_moves)
    parts, far_cuts, far_values = refs[:count], refs[count : count + far], refs[count + far : count + 2 * far]
    out_ref, *far_outs, sems = refs[count + 2 * far :]
    feats = out_ref.shape[0] // (count + far)

    def send(index, move, part):
        rows = pl.ds(pl.multiple_of(owner((-move[0], move[1])) * feats, feats), feats)
        copy = pltpu.make_async_copy(part, out_ref.at[rows, :], sems.at[index])
        copy.start()
        return copy

    copies = [send(index, move, part) for index, (move, part) in enumerate(zip(moves, parts))]
    for index, move in enumerate(far_moves):
        place_blocks([0], far_cuts[index], far_values[index], [far_outs[index]])
        copies.append(send(count + index, move, far_outs[index]))
    for copy in copies:
        copy.wait()


def finish(moves, parts, far_moves, far_cuts, far_values):
    feats, wide = parts[0].shape
    blocks = len(moves) + len(far_moves)
    return pl.pallas_call(
        lambda *refs: finish_kernel(moves, far_moves, *refs),
        in_specs=in_vmem(len(parts) + 2 * len(far_moves)),
        out_specs=pl.BlockSpec(memory_space=pl.ANY),
        out_shape=jax.ShapeDtypeStruct((blocks * feats, wide), jnp.float32),
        scratch_shapes=[pltpu.VMEM((feats, wide), jnp.float32)] * len(far_moves)
        + [pltpu.SemaphoreType.DMA((blocks,))],
        compiler_params=pltpu.CompilerParams(vmem_limit_bytes=16 << 20),
        name="finish",
    )(*parts, *far_cuts, *far_values)


def owner(move):
    me = lax.axis_index("feat")
    return (me // 2 + move[0] + 4) % 4 * 2 + (me % 2 ^ move[1])


def send_feat(array, move):
    return lax.ppermute(array, "feat", [(i, (i // 2 + move[0]) % 4 * 2 + (i % 2 ^ move[1])) for i in range(8)])


def flip_feat(array, flip):
    return lax.ppermute(array, "feat", [(i, i ^ flip) for i in range(8)])


def shift_rows(array, shift):
    return lax.ppermute(array, "rows", [(i, i // 8 * 8 + (i + shift) % 8) for i in range(32)])


def turn_rows(array, turn):
    return lax.ppermute(array, "rows", [(i, (i + 8 * turn) % 32) for i in range(32)])


def on_device(feature_values, hessian_codes, edge_codes, cut_ranks):
    hess_own = hessian_codes.astype(jnp.float32) * (1.0 / 65536.0)
    hess = hess_own.reshape(1, -1)
    slots = {}
    codes, values = edge_codes, feature_values
    for flip, turns in ((1, (1,)), (2, (2,)), (4, (3, 0))):
        other = flip_feat(hess, flip)
        for turn in turns:
            search = find_slots if turn == 1 else find_near_slots
            slots[turn] = search(turn, codes, values)
        hess = jnp.concatenate([hess, other], axis=0)
        if flip < 4:
            hess, slots[turn], codes = lax.optimization_barrier((hess, slots[turn], codes))
    far_moves = [(2, 0), (2, 1)]
    far_blocks, hess = lax.optimization_barrier((cut_blocks(far_moves, feature_values), hess))
    far_values = [send_feat(block, move) for block, move in zip(far_blocks, far_moves)]
    parts = [turn_rows(find_mass(hess, *slots[turn]), turn) for turn in (1, 2, 3)]
    mass = find_mass(hess, *slots[0]) + parts[0] + parts[1] + parts[2]
    before = mass + shift_rows(mass, 1)
    around = before + shift_rows(mass, -1)
    cuts = find_cuts(edge_codes, cut_ranks, around, shift_rows(around, -3), shift_rows(before, 2))
    cuts, far_values = lax.optimization_barrier((cuts, far_values))
    cuts = [cuts] + [turn_rows(cuts, turn) for turn in (1, 2, 3)]
    cuts = collect(cuts)
    far_cuts = [send_feat(cuts, move) for move in far_moves]
    stages = [[(1, 0), (3, 0)], [(1, 1), (3, 1)], [(0, 1)], [(0, 0)]]
    moves, parts = [], []
    for stage in stages:
        outs = place(stage, cuts, feature_values)
        cuts, outs = lax.optimization_barrier((cuts, outs))
        moves += stage
        parts += [send_feat(out, move) if move != (0, 0) else out for out, move in zip(outs, stage)]
    return finish(moves, parts, far_moves, far_cuts, far_values)


def solution(mesh):
    placed = (P("feat", "rows"), P(("rows", "feat")), P("feat", None), P("feat", None))
    return jax.shard_map(
        on_device, mesh=mesh, in_specs=placed, out_specs=P(None, ("rows", "feat")), check_vma=False
    )
```

```python
import jax
import jax.numpy as jnp
from jax import lax
from jax.experimental import pallas as pl
from jax.experimental.pallas import tpu as pltpu
from jax.sharding import PartitionSpec as P

LANES = 128
FEATS = 16
DEPTH = 4
TILE = 256
UNROLL = 8


def in_vmem(count):
    return [pl.BlockSpec(memory_space=pltpu.VMEM)] * count


def lane_take(table, index):
    return jnp.take_along_axis(table, index, axis=1, mode="promise_in_bounds")


def pick_columns(wide, index):
    low = lane_take(wide[:, :LANES], index & (LANES - 1))
    high = lane_take(wide[:, LANES:], index & (LANES - 1))
    return jnp.where(index < LANES, low, high)


def lane_iota(shape):
    return lax.broadcasted_iota(jnp.int32, shape, 1)


def choose(marks, low, high, masks):
    middle = (low + high) // 2
    if not masks:
        return marks[middle]
    upper = choose(marks, middle, high, masks[1:])
    return jnp.where(masks[0], upper, choose(marks, low, middle, masks[1:]))


def spread(even):
    return {i: jnp.broadcast_to(even[:, i : i + 1], even.shape) for i in range(128 >> DEPTH, 128, 128 >> DEPTH)}


def search_pairs(tables, values):
    masks = [[] for _ in values]
    for _ in range(DEPTH):
        for (_, marks), mask, value in zip(tables, masks, values):
            mask.append(value >= choose(marks, 0, LANES, mask))
    bases = []
    for mask in masks:
        base = jnp.where(mask[0], 64, 0)
        for level in range(1, DEPTH):
            base = base + jnp.where(mask[level], 64 >> level, 0)
        bases.append(base)
    step = 64 >> DEPTH
    while step:
        probes = [base + step for base in bases]
        entries = [lane_take(even, probe) for (even, _), probe in zip(tables, probes)]
        bases = [jnp.where(v >= e, p, b) for v, e, p, b in zip(values, entries, probes, bases)]
        step //= 2
    return bases


def even_odd(codes):
    lane = lane_iota((codes.shape[0], LANES))
    edges = codes.astype(jnp.float32) * (1.0 / 256.0)
    return pick_columns(edges, 2 * lane), pick_columns(edges, 2 * lane + 1)


def slot_kernel(group, moves, codes_hbm, values_hbm, top_ref, low_ref, *refs):
    *blocks, codes_ref, values_ref, sems = refs
    rows = values_ref.shape[1]
    wide = blocks[0].shape[1]
    own = slice(group * FEATS, (group + 1) * FEATS)
    span = rows // 2
    copies = [pltpu.make_async_copy(codes_hbm.at[own, :], codes_ref, sems.at[2])]
    for part in range(2):
        at = slice(part * span, (part + 1) * span)
        copies.append(pltpu.make_async_copy(values_hbm.at[own, at], values_ref.at[:, at], sems.at[part]))
    for index, (move, block) in enumerate(zip(moves, blocks)):
        at = pl.ds(pl.multiple_of(owner(move) * wide, wide), wide)
        copies.append(pltpu.make_async_copy(values_hbm.at[:, at], block, sems.at[3 + index]))
    for copy in copies:
        copy.start()
    copies[0].wait()
    for part in range(2):
        copies[1 + part].wait()
        search_slots(0, codes_ref, values_ref, top_ref, low_ref, (part / 2, (part + 1) / 2))
    for copy in copies[3:]:
        copy.wait()


def search_slots(first, codes_ref, values_ref, top_ref, low_ref, share):
    width = 32
    steps = values_ref.shape[1] // (width * LANES)
    tables = []
    for half in range(2):
        at = pl.ds(first + 8 * half, 8)
        even, odd = even_odd(codes_ref[at, :])
        tables.append((at, odd, (even, spread(even))))

    def chunk(step, carry):
        columns = [pl.ds(pl.multiple_of((step * width + part) * LANES, LANES), LANES) for part in range(width)]
        tops, lows = [[] for _ in columns], [[] for _ in columns]
        for at, odd, table in tables:
            values = [values_ref[at, column] for column in columns]
            pairs = search_pairs([table] * width, values)
            entries = [lane_take(odd, pair) for pair in pairs]
            for top, low, value, pair, entry in zip(tops, lows, values, pairs, entries):
                top.append((pair >> 3).astype(jnp.float32))
                low.append((2 * (pair & 7) + jnp.where(value >= entry, 1, 0)).astype(jnp.float32))
        for column, top, low in zip(columns, tops, lows):
            top_ref[:, column] = jnp.concatenate(top, axis=0).astype(jnp.bfloat16)
            low_ref[:, column] = jnp.concatenate(low, axis=0).astype(jnp.bfloat16)
        return carry

    lax.fori_loop(int(share[0] * steps), int(share[1] * steps), chunk, 0)


def near_slot_kernel(groups, codes_ref, values_ref, *refs):
    for index, group in enumerate(groups):
        search_slots(group * FEATS, codes_ref, values_ref, *refs[2 * index : 2 * index + 2], (0, 1))


def find_near_slots(groups, edge_codes, values):
    slots = jax.ShapeDtypeStruct((FEATS, values.shape[1]), jnp.bfloat16)
    return pl.pallas_call(
        lambda *refs: near_slot_kernel(groups, *refs),
        in_specs=in_vmem(2),
        out_specs=in_vmem(2 * len(groups)),
        out_shape=[slots] * (2 * len(groups)),
        compiler_params=pltpu.CompilerParams(vmem_limit_bytes=16 << 20),
        cost_estimate=pl.CostEstimate(flops=10**7, bytes_accessed=10**7, transcendentals=0),
        name="slots",
    )(edge_codes, values)


def find_slots(group, moves, edge_codes, values):
    feats, rows = values.shape
    slots = jax.ShapeDtypeStruct((FEATS, rows), jnp.bfloat16)
    block = jax.ShapeDtypeStruct((feats, rows // 8), jnp.float32)
    return pl.pallas_call(
        lambda *refs: slot_kernel(group, moves, *refs),
        in_specs=[pl.BlockSpec(memory_space=pltpu.HBM)] * 2,
        out_specs=in_vmem(2 + len(moves)),
        out_shape=[slots] * 2 + [block] * len(moves),
        scratch_shapes=[
            pltpu.VMEM((FEATS, 256), jnp.int32),
            pltpu.VMEM((FEATS, rows), jnp.float32),
            pltpu.SemaphoreType.DMA((3 + len(moves),)),
        ],
        compiler_params=pltpu.CompilerParams(vmem_limit_bytes=16 << 20),
        cost_estimate=pl.CostEstimate(flops=10**7, bytes_accessed=10**7, transcendentals=0),
        name="slots",
    )(
        pltpu.with_memory_space_constraint(edge_codes, pltpu.HBM),
        pltpu.with_memory_space_constraint(values, pltpu.HBM),
    )


def hist_kernel(hess_ref, *refs):
    *slots, mass_ref, high_ref, rest_ref, sum_ref = refs
    rows = slots[0].shape[1]
    scaled = hess_ref[...] * 65536.0
    high = jnp.floor(scaled * (1.0 / 256.0))
    rest = scaled - high * 256.0
    wide = hess_ref.shape[1]
    me = lax.axis_index("feat")
    for part in range(rows // wide):
        own = pl.ds(pl.multiple_of((part ^ me) * wide, wide), wide)
        high_ref[:, own] = jnp.broadcast_to(high[part : part + 1], (FEATS, wide)).astype(jnp.bfloat16)
        rest_ref[:, own] = jnp.broadcast_to(rest[part : part + 1], (FEATS, wide)).astype(jnp.bfloat16)

    for group in range(len(slots) // 2):
        hist_group(group, *slots[2 * group : 2 * group + 2], mass_ref, high_ref, rest_ref, sum_ref)


def hist_group(group, top_ref, low_ref, mass_ref, high_ref, rest_ref, sum_ref):
    rows = top_ref.shape[1]
    shape = (FEATS, LANES)
    lane = lane_iota(shape)
    feat = lax.broadcasted_iota(jnp.int32, shape, 0)

    def multiply(*sums):
        zero = jnp.zeros((FEATS, TILE), jnp.bfloat16)
        one = jnp.ones((FEATS, TILE), jnp.bfloat16)
        units = (sums[:16], sums[16:])

        def step(index, carry):
            for turn in range(UNROLL):
                spots = [pl.ds(pl.multiple_of(((index * UNROLL + turn) * 2 + unit) * TILE, TILE), TILE) for unit in range(2)]
                for unit, at in enumerate(spots):
                    low = low_ref[:, at]
                    below = jnp.concatenate([jnp.where(low <= k, one, zero) for k in range(16)], axis=0)
                    pltpu.matmul_push_rhs(below, turn % 2, unit, transpose=True)
                for unit, at in enumerate(spots):
                    top, w_high, w_rest = top_ref[:, at], high_ref[:, at], rest_ref[:, at]
                    for k in range(16):
                        hit = top == k
                        weighted = jnp.concatenate([jnp.where(hit, w_high, zero), jnp.where(hit, w_rest, zero)], axis=0)
                        pltpu.matmul_acc_lhs(units[unit][k], weighted, load_staged_rhs=turn % 2 if k == 0 else None)
            return carry

        lax.fori_loop(0, rows // (2 * TILE * UNROLL), step, 0)
        for k in range(16):
            both = pltpu.matmul_pop(units[0][k]) + pltpu.matmul_pop(units[1][k])
            sum_ref[k * FEATS : (k + 1) * FEATS] = both[:FEATS] * (1.0 / 256.0) + both[FEATS:] * (1.0 / 65536.0)

    pl.run_scoped(multiply, *[pltpu.ACC(mxu_id=unit)((2 * FEATS, TILE), jnp.float32) for unit in range(2) for _ in range(16)])

    points = [2 * lane - 1, 2 * lane]
    columns = [(point & 7) * FEATS + feat for point in points]
    results = [jnp.zeros(shape, jnp.float32)] * 2
    before = jnp.zeros(shape, jnp.float32)
    for k in range(16):
        block = sum_ref[k * FEATS : (k + 1) * FEATS]
        for parity, (point, column) in enumerate(zip(points, columns)):
            here = jnp.where((point & 15) < 8, lane_take(block[:, :LANES], column), lane_take(block[:, LANES:], column))
            results[parity] = jnp.where((point >> 4) == k, before + here, results[parity])
        before = before + lane_take(block[:, LANES:], 7 * FEATS + feat)
    own = slice(group * FEATS, (group + 1) * FEATS)
    mass_ref[own, :LANES] = results[0]
    mass_ref[own, LANES:] = results[1]


def find_mass(hess, slots):
    rows = slots[0].shape[1]
    feats = FEATS * len(slots) // 2
    return pl.pallas_call(
        hist_kernel,
        in_specs=in_vmem(1 + len(slots)),
        out_specs=in_vmem(1)[0],
        out_shape=jax.ShapeDtypeStruct((feats, 256), jnp.float32),
        scratch_shapes=[pltpu.VMEM((FEATS, rows), jnp.bfloat16)] * 2
        + [pltpu.VMEM((16 * FEATS, TILE), jnp.float32)],
        compiler_params=pltpu.CompilerParams(vmem_limit_bytes=24 << 20),
        cost_estimate=pl.CostEstimate(flops=4 * 10**9, bytes_accessed=10**7, transcendentals=0),
        name="hist",
    )(hess, *slots)


def cuts_kernel(codes_ref, ranks_ref, *refs):
    *mass_refs, cuts_ref = refs

    def step(group, carry):
        at = pl.ds(pl.multiple_of(group * FEATS, FEATS), FEATS)
        mass = mass_refs[0][at, :]
        for mass_ref in mass_refs[1:]:
            mass = mass + mass_ref[at, :]
        cut_group(at, codes_ref, ranks_ref, mass, cuts_ref)
        return carry

    lax.fori_loop(0, codes_ref.shape[0] // FEATS, step, 0)


def cut_group(at, codes_ref, ranks_ref, mass, cuts_ref):
    shape = (FEATS, LANES)
    lane = lane_iota(shape)
    edge_even, edge_odd = even_odd(codes_ref[at, :])
    edge_next = lane_take(edge_even, (lane + 1) & (LANES - 1))
    mass_even, mass_odd = mass[:, :LANES], mass[:, LANES:]
    mass_next = lane_take(mass_even, (lane + 1) & (LANES - 1))
    total = jnp.broadcast_to(mass_odd[:, LANES - 1 :], shape)
    ranks = ranks_ref[at, :].astype(jnp.float32)
    orders = [jnp.where(lane == 0, 255, 2 * lane - 1), 2 * lane]
    targets = [pick_columns(ranks, order) * (1.0 / 65792.0) * total for order in orders]
    pairs = search_pairs([(mass_even, spread(mass_even))] * 2, targets)
    for side, (target, pair) in enumerate(zip(targets, pairs)):
        mid_mass = lane_take(mass_odd, pair)
        mid_edge = lane_take(edge_odd, pair)
        above = target >= mid_mass
        low_mass = jnp.where(above, mid_mass, lane_take(mass_even, pair))
        high_mass = jnp.where(above, lane_take(mass_next, pair), mid_mass)
        low_edge = jnp.where(above, mid_edge, lane_take(edge_even, pair))
        high_edge = jnp.where(above, lane_take(edge_next, pair), mid_edge)
        part = (target - low_mass) / (high_mass - low_mass)
        cuts_ref[at, side * LANES : (side + 1) * LANES] = low_edge + part * (high_edge - low_edge)


def find_cuts(edge_codes, cut_ranks, *sums):
    return pl.pallas_call(
        cuts_kernel,
        in_specs=in_vmem(2 + len(sums)),
        out_specs=in_vmem(1)[0],
        out_shape=jax.ShapeDtypeStruct((edge_codes.shape[0], 256), jnp.float32),
        compiler_params=pltpu.CompilerParams(vmem_limit_bytes=4 << 20),
        name="cuts",
    )(edge_codes, cut_ranks, *sums)


def place_groups(groups):
    tables, all_values, rest = [], [], []
    for raw, odd, values, writes in groups:
        shape = odd.shape
        lane = lane_iota(shape)
        last = jnp.broadcast_to(raw[:, :1], shape)
        even = jnp.where(lane == 0, -16.0, raw)
        after = jnp.where(lane == LANES - 1, last, lane_take(even, (lane + 1) & (LANES - 1)))
        inv_low = 1.0 / (odd - even)
        inv_high = 1.0 / (after - odd)
        inv_last = 1.0 / (16.0 - last)
        tables += [(even, spread(even))] * len(values)
        all_values += values
        rest += [(odd, inv_low, inv_high, last, inv_last, write) for write in writes]
    pairs = search_pairs(tables, all_values)
    knots = [lane_take(item[0], pair) for item, pair in zip(rest, pairs)]
    lows = [lane_take(item[1], pair) for item, pair in zip(rest, pairs)]
    highs = [lane_take(item[2], pair) for item, pair in zip(rest, pairs)]
    for item, value, pair, knot, low, high in zip(rest, all_values, pairs, knots, lows, highs):
        last, inv_last, write = item[3:]
        inside = (2 * pair + 1).astype(jnp.float32) + (value - knot) * jnp.where(value >= knot, high, low)
        write(jnp.where(value >= last, 256.0 + (value - last) * inv_last, inside))


def place_kernel(moves, cuts_ref, values_ref, *out_refs):
    wide = out_refs[0].shape[1]
    place_blocks([owner(move) * wide for move in moves], cuts_ref, values_ref, out_refs)


def place_blocks(bases, cuts_ref, values_ref, out_refs):
    feats, wide = out_refs[0].shape
    together = 4

    def store(out_ref, at, part):
        def write(value):
            out_ref[at, part : part + LANES] = value

        return write

    def step(index, carry):
        groups = []
        for turn in range(together):
            at = pl.ds(pl.multiple_of((index * together + turn) * 8, 8), 8)
            values, writes = [], []
            for base, out_ref in zip(bases, out_refs):
                for part in range(0, wide, LANES):
                    values.append(values_ref[at, pl.ds(pl.multiple_of(base + part, LANES), LANES)])
                    writes.append(store(out_ref, at, part))
            groups.append((cuts_ref[at, :LANES], cuts_ref[at, LANES:], values, writes))
        place_groups(groups)
        return carry

    lax.fori_loop(0, feats // (8 * together), step, 0)


def place(moves, cuts, values):
    feats, rows = values.shape
    block = jax.ShapeDtypeStruct((feats, rows // 8), jnp.float32)
    return pl.pallas_call(
        lambda *refs: place_kernel(moves, *refs),
        in_specs=in_vmem(2),
        out_specs=in_vmem(len(moves)),
        out_shape=[block] * len(moves),
        compiler_params=pltpu.CompilerParams(vmem_limit_bytes=16 << 20),
        cost_estimate=pl.CostEstimate(flops=10**5, bytes_accessed=10**4, transcendentals=0),
        name="place",
    )(cuts, values)


def far_kernel(*refs):
    count = len(refs) // 3
    for cuts_ref, values_ref, out_ref in zip(refs[:count], refs[count : 2 * count], refs[2 * count :]):
        place_blocks([0], cuts_ref, values_ref, [out_ref])


def place_far(cuts, values):
    return pl.pallas_call(
        far_kernel,
        in_specs=in_vmem(2 * len(cuts)),
        out_specs=in_vmem(len(cuts)),
        out_shape=[jax.ShapeDtypeStruct(block.shape, jnp.float32) for block in values],
        compiler_params=pltpu.CompilerParams(vmem_limit_bytes=16 << 20),
        cost_estimate=pl.CostEstimate(flops=10**5, bytes_accessed=10**4, transcendentals=0),
        name="far",
    )(*cuts, *values)


def join_kernel(moves, *refs):
    *parts, out_ref, sems = refs
    feats = parts[0].shape[0]
    copies = []
    for index, (move, part) in enumerate(zip(moves, parts)):
        rows = pl.ds(pl.multiple_of(owner((-move[0], move[1])) * feats, feats), feats)
        copies.append(pltpu.make_async_copy(part, out_ref.at[rows, :], sems.at[index]))
    for copy in copies:
        copy.start()
    for copy in copies:
        copy.wait()


def join(moves, parts):
    feats, wide = parts[0].shape
    return pl.pallas_call(
        lambda *refs: join_kernel(moves, *refs),
        in_specs=in_vmem(len(parts)),
        out_specs=pl.BlockSpec(memory_space=pl.ANY),
        out_shape=jax.ShapeDtypeStruct((len(parts) * feats, wide), jnp.float32),
        scratch_shapes=[pltpu.SemaphoreType.DMA((len(parts),))],
        compiler_params=pltpu.CompilerParams(vmem_limit_bytes=4 << 20),
        name="join",
    )(*parts)


def owner(move):
    me = lax.axis_index("feat")
    return (me // 2 + move[0] + 4) % 4 * 2 + (me % 2 ^ move[1])


def send_feat(array, move):
    return lax.ppermute(array, "feat", [(i, (i // 2 + move[0]) % 4 * 2 + (i % 2 ^ move[1])) for i in range(8)])


def flip_feat(array, flip):
    return lax.ppermute(array, "feat", [(i, i ^ flip) for i in range(8)])


def shift_rows(array, shift):
    return lax.ppermute(array, "rows", [(i, i // 8 * 8 + (i + shift) % 8) for i in range(32)])


def turn_rows(array, turn):
    return lax.ppermute(array, "rows", [(i, (i + 8 * turn) % 32) for i in range(32)])


def on_device(feature_values, hessian_codes, edge_codes, cut_ranks):
    hess_own = hessian_codes.astype(jnp.float32) * (1.0 / 65536.0)
    hess = hess_own.reshape(1, -1)
    far_moves = [(2, 0), (2, 1)]
    codes, slots = edge_codes, []
    for flip, groups in ((1, (0,)), (2, (1,)), (4, (2, 3))):
        other = flip_feat(hess, flip)
        if flip == 1:
            top, low, *far_blocks = find_slots(0, far_moves, codes, feature_values)
            slots += [top, low]
        else:
            slots += find_near_slots(groups, codes, feature_values)
        hess = jnp.concatenate([hess, other], axis=0)
        if flip < 4:
            hess, slots, codes = lax.optimization_barrier((hess, slots, codes))
    far_blocks, hess = lax.optimization_barrier((far_blocks, hess))
    far_values = [send_feat(block, move) for block, move in zip(far_blocks, far_moves)]
    mass = find_mass(hess, slots)
    before = mass + shift_rows(mass, 1)
    around = before + shift_rows(mass, -1)
    mass = around + shift_rows(around, -3) + shift_rows(before, 2)
    cuts = find_cuts(edge_codes, cut_ranks, mass, *[turn_rows(mass, turn) for turn in (1, 2, 3)])
    cuts, far_values = lax.optimization_barrier((cuts, far_values))
    far_cuts = [send_feat(cuts, move) for move in far_moves]
    stages = [[(1, 0), (3, 0)], [(1, 1), (3, 1)], [(0, 1)], [(0, 0)]]
    moves, parts = [], []
    for stage in stages:
        outs = place(stage, cuts, feature_values)
        if stage[0] == (1, 1):
            cuts, outs, far_cuts = lax.optimization_barrier((cuts, outs, far_cuts))
        elif stage[0] == (0, 1):
            cuts, outs, far_cuts, far_values = lax.optimization_barrier((cuts, outs, far_cuts, far_values))
        else:
            cuts, outs = lax.optimization_barrier((cuts, outs))
        moves += stage
        parts += [send_feat(out, move) if move != (0, 0) else out for out, move in zip(outs, stage)]
    return join(moves + far_moves, parts + list(place_far(far_cuts, far_values)))


def solution(mesh):
    placed = (P("feat", "rows"), P(("rows", "feat")), P("feat", None), P("feat", None))
    return jax.shard_map(
        on_device, mesh=mesh, in_specs=placed, out_specs=P(None, ("rows", "feat")), check_vma=False
    )
```

```python
import jax
import jax.numpy as jnp
from jax import lax
from jax.experimental import pallas as pl
from jax.experimental.pallas import tpu as pltpu
from jax.sharding import PartitionSpec as P

LANES = 128
FEATS = 16
DEPTH = 4
TILE = 256
UNROLL = 8


def in_vmem(count):
    return [pl.BlockSpec(memory_space=pltpu.VMEM)] * count


def lane_take(table, index):
    return jnp.take_along_axis(table, index, axis=1, mode="promise_in_bounds")


def pick_columns(wide, index):
    low = lane_take(wide[:, :LANES], index & (LANES - 1))
    high = lane_take(wide[:, LANES:], index & (LANES - 1))
    return jnp.where(index < LANES, low, high)


def lane_iota(shape):
    return lax.broadcasted_iota(jnp.int32, shape, 1)


def choose(marks, low, high, masks):
    middle = (low + high) // 2
    if not masks:
        return marks[middle]
    upper = choose(marks, middle, high, masks[1:])
    return jnp.where(masks[0], upper, choose(marks, low, middle, masks[1:]))


def spread(even):
    return {i: jnp.broadcast_to(even[:, i : i + 1], even.shape) for i in range(128 >> DEPTH, 128, 128 >> DEPTH)}


def search_pairs(tables, values):
    masks = [[] for _ in values]
    for _ in range(DEPTH):
        for (_, marks), mask, value in zip(tables, masks, values):
            mask.append(value >= choose(marks, 0, LANES, mask))
    bases = []
    for mask in masks:
        base = jnp.where(mask[0], 64, 0)
        for level in range(1, DEPTH):
            base = base + jnp.where(mask[level], 64 >> level, 0)
        bases.append(base)
    step = 64 >> DEPTH
    while step:
        probes = [base + step for base in bases]
        entries = [lane_take(even, probe) for (even, _), probe in zip(tables, probes)]
        bases = [jnp.where(v >= e, p, b) for v, e, p, b in zip(values, entries, probes, bases)]
        step //= 2
    return bases


def even_odd(codes):
    lane = lane_iota((codes.shape[0], LANES))
    edges = codes.astype(jnp.float32) * (1.0 / 256.0)
    return pick_columns(edges, 2 * lane), pick_columns(edges, 2 * lane + 1)


def slot_kernel(group, moves, codes_hbm, values_hbm, top_ref, low_ref, *refs):
    *blocks, codes_ref, values_ref, sems = refs
    rows = values_ref.shape[1]
    wide = blocks[0].shape[1]
    own = slice(group * FEATS, (group + 1) * FEATS)
    span = rows // 2
    copies = [pltpu.make_async_copy(codes_hbm.at[own, :], codes_ref, sems.at[2])]
    for part in range(2):
        at = slice(part * span, (part + 1) * span)
        copies.append(pltpu.make_async_copy(values_hbm.at[own, at], values_ref.at[:, at], sems.at[part]))
    for index, (move, block) in enumerate(zip(moves, blocks)):
        at = pl.ds(pl.multiple_of(owner(move) * wide, wide), wide)
        copies.append(pltpu.make_async_copy(values_hbm.at[:, at], block, sems.at[3 + index]))
    for copy in copies:
        copy.start()
    copies[0].wait()
    for part in range(2):
        copies[1 + part].wait()
        search_slots(0, codes_ref, values_ref, top_ref, low_ref, (part / 2, (part + 1) / 2))
    for copy in copies[3:]:
        copy.wait()


def search_slots(first, codes_ref, values_ref, top_ref, low_ref, share):
    width = 32
    steps = values_ref.shape[1] // (width * LANES)
    tables = []
    for half in range(2):
        at = pl.ds(first + 8 * half, 8)
        even, odd = even_odd(codes_ref[at, :])
        tables.append((at, odd, (even, spread(even))))

    def chunk(step, carry):
        columns = [pl.ds(pl.multiple_of((step * width + part) * LANES, LANES), LANES) for part in range(width)]
        tops, lows = [[] for _ in columns], [[] for _ in columns]
        for at, odd, table in tables:
            values = [values_ref[at, column] for column in columns]
            pairs = search_pairs([table] * width, values)
            entries = [lane_take(odd, pair) for pair in pairs]
            for top, low, value, pair, entry in zip(tops, lows, values, pairs, entries):
                top.append((pair >> 3).astype(jnp.float32))
                low.append((2 * (pair & 7) + jnp.where(value >= entry, 1, 0)).astype(jnp.float32))
        for column, top, low in zip(columns, tops, lows):
            top_ref[:, column] = jnp.concatenate(top, axis=0).astype(jnp.bfloat16)
            low_ref[:, column] = jnp.concatenate(low, axis=0).astype(jnp.bfloat16)
        return carry

    lax.fori_loop(int(share[0] * steps), int(share[1] * steps), chunk, 0)


def near_slot_kernel(groups, codes_ref, values_ref, *refs):
    for index, group in enumerate(groups):
        search_slots(group * FEATS, codes_ref, values_ref, *refs[2 * index : 2 * index + 2], (0, 1))


def find_near_slots(groups, edge_codes, values):
    slots = jax.ShapeDtypeStruct((FEATS, values.shape[1]), jnp.bfloat16)
    return pl.pallas_call(
        lambda *refs: near_slot_kernel(groups, *refs),
        in_specs=in_vmem(2),
        out_specs=in_vmem(2 * len(groups)),
        out_shape=[slots] * (2 * len(groups)),
        compiler_params=pltpu.CompilerParams(vmem_limit_bytes=16 << 20),
        cost_estimate=pl.CostEstimate(flops=10**7, bytes_accessed=10**7, transcendentals=0),
        name="slots",
    )(edge_codes, values)


def find_slots(group, moves, edge_codes, values):
    feats, rows = values.shape
    slots = jax.ShapeDtypeStruct((FEATS, rows), jnp.bfloat16)
    block = jax.ShapeDtypeStruct((feats, rows // 8), jnp.float32)
    return pl.pallas_call(
        lambda *refs: slot_kernel(group, moves, *refs),
        in_specs=[pl.BlockSpec(memory_space=pltpu.HBM)] * 2,
        out_specs=in_vmem(2 + len(moves)),
        out_shape=[slots] * 2 + [block] * len(moves),
        scratch_shapes=[
            pltpu.VMEM((FEATS, 256), jnp.int32),
            pltpu.VMEM((FEATS, rows), jnp.float32),
            pltpu.SemaphoreType.DMA((3 + len(moves),)),
        ],
        compiler_params=pltpu.CompilerParams(vmem_limit_bytes=16 << 20),
        cost_estimate=pl.CostEstimate(flops=10**7, bytes_accessed=10**7, transcendentals=0),
        name="slots",
    )(
        pltpu.with_memory_space_constraint(edge_codes, pltpu.HBM),
        pltpu.with_memory_space_constraint(values, pltpu.HBM),
    )


def factor_kernel(codes_hbm, out_ref, codes_ref, sem):
    copy = pltpu.make_async_copy(codes_hbm, codes_ref, sem)
    copy.start()
    copy.wait()
    weight = codes_ref[...].astype(jnp.float32)
    first = jnp.ones_like(weight)
    second = weight.astype(jnp.bfloat16).astype(jnp.float32)
    error = jnp.abs(second - weight)
    for index in range(1, 128):
        left = 1.0 + index / 128.0
        right = (weight * (1.0 / left)).astype(jnp.bfloat16).astype(jnp.float32)
        off = jnp.abs(left * right - weight)
        better = off < error
        error = jnp.minimum(off, error)
        first = jnp.where(better, left, first)
        second = jnp.where(better, right, second)
    out_ref[0] = first
    out_ref[1] = second * (1.0 / 65536.0)


def factor_weights(codes):
    return pl.pallas_call(
        factor_kernel,
        in_specs=[pl.BlockSpec(memory_space=pltpu.HBM)],
        out_specs=in_vmem(1)[0],
        out_shape=jax.ShapeDtypeStruct((2,) + codes.shape, jnp.float32),
        scratch_shapes=[pltpu.VMEM(codes.shape, jnp.int32), pltpu.SemaphoreType.DMA],
        compiler_params=pltpu.CompilerParams(vmem_limit_bytes=4 << 20),
        name="factor",
    )(pltpu.with_memory_space_constraint(codes, pltpu.HBM))


def hist_kernel(hess_ref, *refs):
    *slots, mass_ref, first_ref, second_ref, sum_ref = refs
    blocks, tiles, lanes = hess_ref.shape
    wide = tiles * lanes
    me = lax.axis_index("feat")
    for block in range(blocks // 2):
        for tile in range(tiles):
            own = pl.ds(pl.multiple_of((block ^ me) * wide + tile * lanes, lanes), lanes)
            for ref, part in ((first_ref, 0), (second_ref, 1)):
                row = hess_ref[2 * block + part, tile : tile + 1, :]
                ref[:, own] = jnp.broadcast_to(row, (FEATS, lanes)).astype(jnp.bfloat16)

    for group in range(len(slots) // 2):
        hist_group(group, *slots[2 * group : 2 * group + 2], mass_ref, first_ref, second_ref, sum_ref)


def hist_group(group, top_ref, low_ref, mass_ref, first_ref, second_ref, sum_ref):
    rows = top_ref.shape[1]
    shape = (FEATS, LANES)
    lane = lane_iota(shape)
    feat = lax.broadcasted_iota(jnp.int32, shape, 0)

    def multiply(*sums):
        zero = jnp.zeros((FEATS, TILE), jnp.bfloat16)
        units = (sums[:16], sums[16:])

        def step(index, carry):
            for turn in range(UNROLL):
                spots = [pl.ds(pl.multiple_of(((index * UNROLL + turn) * 2 + unit) * TILE, TILE), TILE) for unit in range(2)]
                for unit, at in enumerate(spots):
                    low, second = low_ref[:, at], second_ref[:, at]
                    below = jnp.concatenate([jnp.where(low <= k, second, zero) for k in range(16)], axis=0)
                    pltpu.matmul_push_rhs(below, turn % 2, unit, transpose=True)
                for unit, at in enumerate(spots):
                    top, first = top_ref[:, at], first_ref[:, at]
                    for k in range(16):
                        weighted = jnp.where(top == k, first, zero)
                        pltpu.matmul_acc_lhs(units[unit][k], weighted, load_staged_rhs=turn % 2 if k == 0 else None)
            return carry

        lax.fori_loop(0, rows // (2 * TILE * UNROLL), step, 0)
        for k in range(16):
            sum_ref[k * FEATS : (k + 1) * FEATS] = pltpu.matmul_pop(units[0][k]) + pltpu.matmul_pop(units[1][k])

    pl.run_scoped(multiply, *[pltpu.ACC(mxu_id=unit)((FEATS, TILE), jnp.float32) for unit in range(2) for _ in range(16)])

    points = [2 * lane - 1, 2 * lane]
    columns = [(point & 7) * FEATS + feat for point in points]
    results = [jnp.zeros(shape, jnp.float32)] * 2
    before = jnp.zeros(shape, jnp.float32)
    for k in range(16):
        block = sum_ref[k * FEATS : (k + 1) * FEATS]
        for parity, (point, column) in enumerate(zip(points, columns)):
            here = jnp.where((point & 15) < 8, lane_take(block[:, :LANES], column), lane_take(block[:, LANES:], column))
            results[parity] = jnp.where((point >> 4) == k, before + here, results[parity])
        before = before + lane_take(block[:, LANES:], 7 * FEATS + feat)
    own = slice(group * FEATS, (group + 1) * FEATS)
    mass_ref[own, :LANES] = results[0]
    mass_ref[own, LANES:] = results[1]


def find_mass(hess, slots):
    rows = slots[0].shape[1]
    feats = FEATS * len(slots) // 2
    return pl.pallas_call(
        hist_kernel,
        in_specs=in_vmem(1 + len(slots)),
        out_specs=in_vmem(1)[0],
        out_shape=jax.ShapeDtypeStruct((feats, 256), jnp.float32),
        scratch_shapes=[pltpu.VMEM((FEATS, rows), jnp.bfloat16)] * 2
        + [pltpu.VMEM((16 * FEATS, TILE), jnp.float32)],
        compiler_params=pltpu.CompilerParams(vmem_limit_bytes=24 << 20),
        cost_estimate=pl.CostEstimate(flops=4 * 10**9, bytes_accessed=10**7, transcendentals=0),
        name="hist",
    )(hess, *slots)


def cuts_kernel(codes_ref, ranks_ref, *refs):
    *mass_refs, cuts_ref = refs

    together = 32

    def step(group, carry):
        at = pl.ds(pl.multiple_of(group * together, together), together)
        mass = mass_refs[0][at, :]
        for mass_ref in mass_refs[1:]:
            mass = mass + mass_ref[at, :]
        cut_group(at, codes_ref, ranks_ref, mass, cuts_ref)
        return carry

    lax.fori_loop(0, codes_ref.shape[0] // together, step, 0)


def cut_group(at, codes_ref, ranks_ref, mass, cuts_ref):
    shape = (mass.shape[0], LANES)
    lane = lane_iota(shape)
    edge_even, edge_odd = even_odd(codes_ref[at, :])
    edge_next = lane_take(edge_even, (lane + 1) & (LANES - 1))
    mass_even, mass_odd = mass[:, :LANES], mass[:, LANES:]
    mass_next = lane_take(mass_even, (lane + 1) & (LANES - 1))
    total = jnp.broadcast_to(mass_odd[:, LANES - 1 :], shape)
    ranks = ranks_ref[at, :].astype(jnp.float32)
    orders = [jnp.where(lane == 0, 255, 2 * lane - 1), 2 * lane]
    targets = [pick_columns(ranks, order) * (1.0 / 65792.0) * total for order in orders]
    pairs = search_pairs([(mass_even, spread(mass_even))] * 2, targets)
    for side, (target, pair) in enumerate(zip(targets, pairs)):
        mid_mass = lane_take(mass_odd, pair)
        mid_edge = lane_take(edge_odd, pair)
        above = target >= mid_mass
        low_mass = jnp.where(above, mid_mass, lane_take(mass_even, pair))
        high_mass = jnp.where(above, lane_take(mass_next, pair), mid_mass)
        low_edge = jnp.where(above, mid_edge, lane_take(edge_even, pair))
        high_edge = jnp.where(above, lane_take(edge_next, pair), mid_edge)
        part = (target - low_mass) / (high_mass - low_mass)
        cuts_ref[at, side * LANES : (side + 1) * LANES] = low_edge + part * (high_edge - low_edge)


def find_cuts(edge_codes, cut_ranks, *sums):
    return pl.pallas_call(
        cuts_kernel,
        in_specs=in_vmem(2 + len(sums)),
        out_specs=in_vmem(1)[0],
        out_shape=jax.ShapeDtypeStruct((edge_codes.shape[0], 256), jnp.float32),
        compiler_params=pltpu.CompilerParams(vmem_limit_bytes=4 << 20),
        name="cuts",
    )(edge_codes, cut_ranks, *sums)


def place_groups(groups):
    tables, all_values, rest = [], [], []
    for raw, odd, values, writes in groups:
        shape = odd.shape
        lane = lane_iota(shape)
        last = jnp.broadcast_to(raw[:, :1], shape)
        even = jnp.where(lane == 0, -16.0, raw)
        after = jnp.where(lane == LANES - 1, last, lane_take(even, (lane + 1) & (LANES - 1)))
        inv_low = 1.0 / (odd - even)
        inv_high = 1.0 / (after - odd)
        inv_last = 1.0 / (16.0 - last)
        tables += [(even, spread(even))] * len(values)
        all_values += values
        rest += [(odd, inv_low, inv_high, last, inv_last, write) for write in writes]
    pairs = search_pairs(tables, all_values)
    knots = [lane_take(item[0], pair) for item, pair in zip(rest, pairs)]
    lows = [lane_take(item[1], pair) for item, pair in zip(rest, pairs)]
    highs = [lane_take(item[2], pair) for item, pair in zip(rest, pairs)]
    for item, value, pair, knot, low, high in zip(rest, all_values, pairs, knots, lows, highs):
        last, inv_last, write = item[3:]
        inside = (2 * pair + 1).astype(jnp.float32) + (value - knot) * jnp.where(value >= knot, high, low)
        write(jnp.where(value >= last, 256.0 + (value - last) * inv_last, inside))


def place_kernel(moves, cuts_ref, values_ref, *out_refs):
    wide = out_refs[0].shape[1]
    place_blocks([owner(move) * wide for move in moves], cuts_ref, values_ref, out_refs)


def place_blocks(bases, cuts_ref, values_ref, out_refs):
    feats, wide = out_refs[0].shape
    together = 4

    def store(out_ref, at, part):
        def write(value):
            out_ref[at, part : part + LANES] = value

        return write

    def step(index, carry):
        groups = []
        for turn in range(together):
            at = pl.ds(pl.multiple_of((index * together + turn) * 8, 8), 8)
            values, writes = [], []
            for base, out_ref in zip(bases, out_refs):
                for part in range(0, wide, LANES):
                    values.append(values_ref[at, pl.ds(pl.multiple_of(base + part, LANES), LANES)])
                    writes.append(store(out_ref, at, part))
            groups.append((cuts_ref[at, :LANES], cuts_ref[at, LANES:], values, writes))
        place_groups(groups)
        return carry

    lax.fori_loop(0, feats // (8 * together), step, 0)


def place(moves, cuts, values):
    feats, rows = values.shape
    block = jax.ShapeDtypeStruct((feats, rows // 8), jnp.float32)
    return pl.pallas_call(
        lambda *refs: place_kernel(moves, *refs),
        in_specs=in_vmem(2),
        out_specs=in_vmem(len(moves)),
        out_shape=[block] * len(moves),
        compiler_params=pltpu.CompilerParams(vmem_limit_bytes=16 << 20),
        cost_estimate=pl.CostEstimate(flops=10**5, bytes_accessed=10**4, transcendentals=0),
        name="place",
    )(cuts, values)


def rest_kernel(cuts_ref, values_ref, *refs):
    count = (len(refs) - 1) // 3
    outs = refs[2 * count :]
    for far_cuts, far_values, out_ref in zip(refs[:count], refs[count : 2 * count], outs):
        place_blocks([0], far_cuts, far_values, [out_ref])
    place_blocks([owner((0, 0)) * outs[count].shape[1]], cuts_ref, values_ref, [outs[count]])


def place_rest(cuts, values, far_cuts, far_values):
    block = jax.ShapeDtypeStruct(far_values[0].shape, jnp.float32)
    return pl.pallas_call(
        rest_kernel,
        in_specs=in_vmem(2 + 2 * len(far_cuts)),
        out_specs=in_vmem(len(far_cuts) + 1),
        out_shape=[block] * (len(far_cuts) + 1),
        compiler_params=pltpu.CompilerParams(vmem_limit_bytes=16 << 20),
        cost_estimate=pl.CostEstimate(flops=10**5, bytes_accessed=10**4, transcendentals=0),
        name="rest",
    )(cuts, values, *far_cuts, *far_values)


def join_kernel(moves, *refs):
    *parts, out_ref, sems = refs
    feats = parts[0].shape[0]
    copies = []
    for index, (move, part) in enumerate(zip(moves, parts)):
        rows = pl.ds(pl.multiple_of(owner((-move[0], move[1])) * feats, feats), feats)
        copies.append(pltpu.make_async_copy(part, out_ref.at[rows, :], sems.at[index]))
    for copy in copies:
        copy.start()
    for copy in copies:
        copy.wait()


def join(moves, parts):
    feats, wide = parts[0].shape
    return pl.pallas_call(
        lambda *refs: join_kernel(moves, *refs),
        in_specs=in_vmem(len(parts)),
        out_specs=pl.BlockSpec(memory_space=pl.ANY),
        out_shape=jax.ShapeDtypeStruct((len(parts) * feats, wide), jnp.float32),
        scratch_shapes=[pltpu.SemaphoreType.DMA((len(parts),))],
        compiler_params=pltpu.CompilerParams(vmem_limit_bytes=4 << 20),
        name="join",
    )(*parts)


def owner(move):
    me = lax.axis_index("feat")
    return (me // 2 + move[0] + 4) % 4 * 2 + (me % 2 ^ move[1])


def send_feat(array, move):
    return lax.ppermute(array, "feat", [(i, (i // 2 + move[0]) % 4 * 2 + (i % 2 ^ move[1])) for i in range(8)])


def flip_feat(array, flip):
    return lax.ppermute(array, "feat", [(i, i ^ flip) for i in range(8)])


def shift_rows(array, shift):
    return lax.ppermute(array, "rows", [(i, i // 8 * 8 + (i + shift) % 8) for i in range(32)])


def turn_rows(array, turn):
    return lax.ppermute(array, "rows", [(i, (i + 8 * turn) % 32) for i in range(32)])


def on_device(feature_values, hessian_codes, edge_codes, cut_ranks):
    hess = factor_weights(hessian_codes.reshape(-1, LANES))
    far_moves = [(2, 0), (2, 1), (0, 1)]
    codes, slots = edge_codes, []
    for flip, groups in ((1, (0,)), (2, (1,)), (4, (2, 3))):
        other = flip_feat(hess, flip)
        if flip == 1:
            top, low, *far_blocks = find_slots(0, far_moves, codes, feature_values)
            slots += [top, low]
        else:
            slots += find_near_slots(groups, codes, feature_values)
        hess = jnp.concatenate([hess, other], axis=0)
        if flip < 4:
            hess, slots, codes = lax.optimization_barrier((hess, slots, codes))
    far_blocks, hess = lax.optimization_barrier((far_blocks, hess))
    far_values = [send_feat(block, move) for block, move in zip(far_blocks, far_moves)]
    mass = find_mass(hess, slots)
    mass, far_values[2] = lax.optimization_barrier((mass, far_values[2]))
    before = mass + shift_rows(mass, 1)
    around = before + shift_rows(mass, -1)
    mass = around + shift_rows(around, -3) + shift_rows(before, 2)
    cuts = find_cuts(edge_codes, cut_ranks, mass, *[turn_rows(mass, turn) for turn in (1, 2, 3)])
    cuts, far_values = lax.optimization_barrier((cuts, far_values))
    far_cuts = [send_feat(cuts, move) for move in far_moves]
    moves, parts = [], []
    for stage in ([(1, 0), (3, 0)], [(1, 1), (3, 1)]):
        outs = place(stage, cuts, feature_values)
        if parts:
            cuts, outs, far_cuts, far_values = lax.optimization_barrier((cuts, outs, far_cuts, far_values))
        else:
            cuts, outs = lax.optimization_barrier((cuts, outs))
        moves += stage
        parts += [send_feat(out, move) for out, move in zip(outs, stage)]
    rest = place_rest(cuts, feature_values, far_cuts, far_values)
    return join(moves + far_moves + [(0, 0)], parts + list(rest))


def solution(mesh):
    placed = (P("feat", "rows"), P(("rows", "feat")), P("feat", None), P("feat", None))
    return jax.shard_map(
        on_device, mesh=mesh, in_specs=placed, out_specs=P(None, ("rows", "feat")), check_vma=False
    )
```

```python
import jax
import jax.numpy as jnp
from jax import lax
from jax.experimental import pallas as pl
from jax.experimental.pallas import tpu as pltpu
from jax.sharding import PartitionSpec as P

LANES = 128
FEATS = 16
DEPTH = 4
TILE = 256
UNROLL = 8


def in_vmem(count):
    return [pl.BlockSpec(memory_space=pltpu.VMEM)] * count


def lane_take(table, index):
    return jnp.take_along_axis(table, index, axis=1, mode="promise_in_bounds")


def pick_columns(wide, index):
    low = lane_take(wide[:, :LANES], index & (LANES - 1))
    high = lane_take(wide[:, LANES:], index & (LANES - 1))
    return jnp.where(index < LANES, low, high)


def lane_iota(shape):
    return lax.broadcasted_iota(jnp.int32, shape, 1)


def choose(marks, low, high, masks):
    middle = (low + high) // 2
    if not masks:
        return marks[middle]
    upper = choose(marks, middle, high, masks[1:])
    return jnp.where(masks[0], upper, choose(marks, low, middle, masks[1:]))


def spread(even):
    return {i: jnp.broadcast_to(even[:, i : i + 1], even.shape) for i in range(128 >> DEPTH, 128, 128 >> DEPTH)}


def search_pairs(tables, values):
    masks = [[] for _ in values]
    for _ in range(DEPTH):
        for (_, marks), mask, value in zip(tables, masks, values):
            mask.append(value >= choose(marks, 0, LANES, mask))
    bases = []
    for mask in masks:
        base = jnp.where(mask[0], 64, 0)
        for level in range(1, DEPTH):
            base = base + jnp.where(mask[level], 64 >> level, 0)
        bases.append(base)
    step = 64 >> DEPTH
    while step:
        probes = [base + step for base in bases]
        entries = [lane_take(even, probe) for (even, _), probe in zip(tables, probes)]
        bases = [jnp.where(v >= e, p, b) for v, e, p, b in zip(values, entries, probes, bases)]
        step //= 2
    return bases


def even_odd(codes):
    lane = lane_iota((codes.shape[0], LANES))
    edges = codes.astype(jnp.float32) * (1.0 / 256.0)
    return pick_columns(edges, 2 * lane), pick_columns(edges, 2 * lane + 1)


def slot_kernel(group, moves, codes_hbm, values_hbm, top_ref, low_ref, *refs):
    *blocks, codes_ref, values_ref, sems = refs
    rows = values_ref.shape[1]
    wide = blocks[0].shape[1]
    own = slice(group * FEATS, (group + 1) * FEATS)
    span = rows // 2
    copies = [pltpu.make_async_copy(codes_hbm.at[own, :], codes_ref, sems.at[2])]
    for part in range(2):
        at = slice(part * span, (part + 1) * span)
        copies.append(pltpu.make_async_copy(values_hbm.at[own, at], values_ref.at[:, at], sems.at[part]))
    for index, (move, block) in enumerate(zip(moves, blocks)):
        at = pl.ds(pl.multiple_of(owner(move) * wide, wide), wide)
        copies.append(pltpu.make_async_copy(values_hbm.at[:, at], block, sems.at[3 + index]))
    for copy in copies:
        copy.start()
    copies[0].wait()
    for part in range(2):
        copies[1 + part].wait()
        search_slots(0, codes_ref, values_ref, top_ref, low_ref, (part / 2, (part + 1) / 2))
    for copy in copies[3:]:
        copy.wait()


def search_slots(first, codes_ref, values_ref, top_ref, low_ref, share):
    width = 32
    steps = values_ref.shape[1] // (width * LANES)
    tables = []
    for half in range(2):
        at = pl.ds(first + 8 * half, 8)
        even, odd = even_odd(codes_ref[at, :])
        tables.append((at, odd, (even, spread(even))))

    def chunk(step, carry):
        columns = [pl.ds(pl.multiple_of((step * width + part) * LANES, LANES), LANES) for part in range(width)]
        tops, lows = [[] for _ in columns], [[] for _ in columns]
        for at, odd, table in tables:
            values = [values_ref[at, column] for column in columns]
            pairs = search_pairs([table] * width, values)
            entries = [lane_take(odd, pair) for pair in pairs]
            for top, low, value, pair, entry in zip(tops, lows, values, pairs, entries):
                top.append((pair >> 3).astype(jnp.float32))
                low.append((2 * (pair & 7) + jnp.where(value >= entry, 1, 0)).astype(jnp.float32))
        for column, top, low in zip(columns, tops, lows):
            top_ref[:, column] = jnp.concatenate(top, axis=0).astype(jnp.bfloat16)
            low_ref[:, column] = jnp.concatenate(low, axis=0).astype(jnp.bfloat16)
        return carry

    lax.fori_loop(int(share[0] * steps), int(share[1] * steps), chunk, 0)


def near_slot_kernel(groups, codes_ref, values_ref, *refs):
    for index, group in enumerate(groups):
        search_slots(group * FEATS, codes_ref, values_ref, *refs[2 * index : 2 * index + 2], (0, 1))


def find_near_slots(groups, edge_codes, values):
    slots = jax.ShapeDtypeStruct((FEATS, values.shape[1]), jnp.bfloat16)
    return pl.pallas_call(
        lambda *refs: near_slot_kernel(groups, *refs),
        in_specs=in_vmem(2),
        out_specs=in_vmem(2 * len(groups)),
        out_shape=[slots] * (2 * len(groups)),
        compiler_params=pltpu.CompilerParams(vmem_limit_bytes=16 << 20),
        cost_estimate=pl.CostEstimate(flops=10**7, bytes_accessed=10**7, transcendentals=0),
        name="slots",
    )(edge_codes, values)


def find_slots(group, moves, edge_codes, values):
    feats, rows = values.shape
    slots = jax.ShapeDtypeStruct((FEATS, rows), jnp.bfloat16)
    block = jax.ShapeDtypeStruct((feats, rows // 8), jnp.float32)
    return pl.pallas_call(
        lambda *refs: slot_kernel(group, moves, *refs),
        in_specs=[pl.BlockSpec(memory_space=pltpu.HBM)] * 2,
        out_specs=in_vmem(2 + len(moves)),
        out_shape=[slots] * 2 + [block] * len(moves),
        scratch_shapes=[
            pltpu.VMEM((FEATS, 256), jnp.int32),
            pltpu.VMEM((FEATS, rows), jnp.float32),
            pltpu.SemaphoreType.DMA((3 + len(moves),)),
        ],
        compiler_params=pltpu.CompilerParams(vmem_limit_bytes=16 << 20),
        cost_estimate=pl.CostEstimate(flops=10**7, bytes_accessed=10**7, transcendentals=0),
        name="slots",
    )(
        pltpu.with_memory_space_constraint(edge_codes, pltpu.HBM),
        pltpu.with_memory_space_constraint(values, pltpu.HBM),
    )


def factor_kernel(codes_hbm, out_ref, codes_ref, sem):
    copy = pltpu.make_async_copy(codes_hbm, codes_ref, sem)
    copy.start()
    copy.wait()
    weight = codes_ref[...].astype(jnp.float32)
    first = jnp.ones_like(weight)
    second = weight.astype(jnp.bfloat16).astype(jnp.float32)
    error = jnp.abs(second - weight)
    for index in range(1, 128):
        left = 1.0 + index / 128.0
        right = (weight * (1.0 / left)).astype(jnp.bfloat16).astype(jnp.float32)
        off = jnp.abs(left * right - weight)
        better = off < error
        error = jnp.minimum(off, error)
        first = jnp.where(better, left, first)
        second = jnp.where(better, right, second)
    out_ref[0] = first
    out_ref[1] = second * (1.0 / 65536.0)


def factor_weights(codes):
    return pl.pallas_call(
        factor_kernel,
        in_specs=[pl.BlockSpec(memory_space=pltpu.HBM)],
        out_specs=in_vmem(1)[0],
        out_shape=jax.ShapeDtypeStruct((2,) + codes.shape, jnp.float32),
        scratch_shapes=[pltpu.VMEM(codes.shape, jnp.int32), pltpu.SemaphoreType.DMA],
        compiler_params=pltpu.CompilerParams(vmem_limit_bytes=4 << 20),
        name="factor",
    )(pltpu.with_memory_space_constraint(codes, pltpu.HBM))


def hist_kernel(hess_ref, *refs):
    *slots, mass_ref, first_ref, second_ref, sum_ref = refs
    blocks, tiles, lanes = hess_ref.shape
    wide = tiles * lanes
    me = lax.axis_index("feat")
    for block in range(blocks // 2):
        for tile in range(tiles):
            own = pl.ds(pl.multiple_of((block ^ me) * wide + tile * lanes, lanes), lanes)
            for ref, part in ((first_ref, 0), (second_ref, 1)):
                row = hess_ref[2 * block + part, tile : tile + 1, :]
                ref[:, own] = jnp.broadcast_to(row, (FEATS, lanes)).astype(jnp.bfloat16)

    for group in range(len(slots) // 2):
        hist_group(group, *slots[2 * group : 2 * group + 2], mass_ref, first_ref, second_ref, sum_ref)


def hist_group(group, top_ref, low_ref, mass_ref, first_ref, second_ref, sum_ref):
    rows = top_ref.shape[1]
    shape = (FEATS, LANES)
    lane = lane_iota(shape)
    feat = lax.broadcasted_iota(jnp.int32, shape, 0)

    def multiply(*sums):
        zero = jnp.zeros((FEATS, TILE), jnp.bfloat16)
        units = (sums[:16], sums[16:])

        def step(index, carry):
            for turn in range(UNROLL):
                spots = [pl.ds(pl.multiple_of(((index * UNROLL + turn) * 2 + unit) * TILE, TILE), TILE) for unit in range(2)]
                for unit, at in enumerate(spots):
                    low, second = low_ref[:, at], second_ref[:, at]
                    below = jnp.concatenate([jnp.where(low <= k, second, zero) for k in range(16)], axis=0)
                    pltpu.matmul_push_rhs(below, turn % 2, unit, transpose=True)
                for unit, at in enumerate(spots):
                    top, first = top_ref[:, at], first_ref[:, at]
                    for k in range(16):
                        weighted = jnp.where(top == k, first, zero)
                        pltpu.matmul_acc_lhs(units[unit][k], weighted, load_staged_rhs=turn % 2 if k == 0 else None)
            return carry

        lax.fori_loop(0, rows // (2 * TILE * UNROLL), step, 0)
        for k in range(16):
            sum_ref[k * FEATS : (k + 1) * FEATS] = pltpu.matmul_pop(units[0][k]) + pltpu.matmul_pop(units[1][k])

    pl.run_scoped(multiply, *[pltpu.ACC(mxu_id=unit)((FEATS, TILE), jnp.float32) for unit in range(2) for _ in range(16)])

    points = [2 * lane - 1, 2 * lane]
    columns = [(point & 7) * FEATS + feat for point in points]
    results = [jnp.zeros(shape, jnp.float32)] * 2
    before = jnp.zeros(shape, jnp.float32)
    for k in range(16):
        block = sum_ref[k * FEATS : (k + 1) * FEATS]
        for parity, (point, column) in enumerate(zip(points, columns)):
            here = jnp.where((point & 15) < 8, lane_take(block[:, :LANES], column), lane_take(block[:, LANES:], column))
            results[parity] = jnp.where((point >> 4) == k, before + here, results[parity])
        before = before + lane_take(block[:, LANES:], 7 * FEATS + feat)
    own = slice(group * FEATS, (group + 1) * FEATS)
    mass_ref[own, :LANES] = results[0]
    mass_ref[own, LANES:] = results[1]


def find_mass(hess, slots):
    rows = slots[0].shape[1]
    feats = FEATS * len(slots) // 2
    return pl.pallas_call(
        hist_kernel,
        in_specs=in_vmem(1 + len(slots)),
        out_specs=in_vmem(1)[0],
        out_shape=jax.ShapeDtypeStruct((feats, 256), jnp.float32),
        scratch_shapes=[pltpu.VMEM((FEATS, rows), jnp.bfloat16)] * 2
        + [pltpu.VMEM((16 * FEATS, TILE), jnp.float32)],
        compiler_params=pltpu.CompilerParams(vmem_limit_bytes=24 << 20),
        cost_estimate=pl.CostEstimate(flops=4 * 10**9, bytes_accessed=10**7, transcendentals=0),
        name="hist",
    )(hess, *slots)


def cuts_kernel(codes_ref, ranks_ref, *refs):
    *mass_refs, cuts_ref = refs

    together = 32

    def step(group, carry):
        at = pl.ds(pl.multiple_of(group * together, together), together)
        mass = mass_refs[0][at, :]
        for mass_ref in mass_refs[1:]:
            mass = mass + mass_ref[at, :]
        cut_group(at, codes_ref, ranks_ref, mass, cuts_ref)
        return carry

    lax.fori_loop(0, codes_ref.shape[0] // together, step, 0)


def cut_group(at, codes_ref, ranks_ref, mass, cuts_ref):
    shape = (mass.shape[0], LANES)
    lane = lane_iota(shape)
    edge_even, edge_odd = even_odd(codes_ref[at, :])
    edge_next = lane_take(edge_even, (lane + 1) & (LANES - 1))
    mass_even, mass_odd = mass[:, :LANES], mass[:, LANES:]
    mass_next = lane_take(mass_even, (lane + 1) & (LANES - 1))
    total = jnp.broadcast_to(mass_odd[:, LANES - 1 :], shape)
    ranks = ranks_ref[at, :].astype(jnp.float32)
    orders = [jnp.where(lane == 0, 255, 2 * lane - 1), 2 * lane]
    targets = [pick_columns(ranks, order) * (1.0 / 65792.0) * total for order in orders]
    pairs = search_pairs([(mass_even, spread(mass_even))] * 2, targets)
    for side, (target, pair) in enumerate(zip(targets, pairs)):
        mid_mass = lane_take(mass_odd, pair)
        mid_edge = lane_take(edge_odd, pair)
        above = target >= mid_mass
        low_mass = jnp.where(above, mid_mass, lane_take(mass_even, pair))
        high_mass = jnp.where(above, lane_take(mass_next, pair), mid_mass)
        low_edge = jnp.where(above, mid_edge, lane_take(edge_even, pair))
        high_edge = jnp.where(above, lane_take(edge_next, pair), mid_edge)
        part = (target - low_mass) / (high_mass - low_mass)
        cuts_ref[at, side * LANES : (side + 1) * LANES] = low_edge + part * (high_edge - low_edge)


def find_cuts(edge_codes, cut_ranks, *sums):
    return pl.pallas_call(
        cuts_kernel,
        in_specs=in_vmem(2 + len(sums)),
        out_specs=in_vmem(1)[0],
        out_shape=jax.ShapeDtypeStruct((edge_codes.shape[0], 256), jnp.float32),
        compiler_params=pltpu.CompilerParams(vmem_limit_bytes=4 << 20),
        name="cuts",
    )(edge_codes, cut_ranks, *sums)


def place_groups(groups):
    tables, all_values, rest = [], [], []
    for raw, odd, values, writes in groups:
        shape = odd.shape
        lane = lane_iota(shape)
        last = jnp.broadcast_to(raw[:, :1], shape)
        even = jnp.where(lane == 0, -16.0, raw)
        after = jnp.where(lane == LANES - 1, last, lane_take(even, (lane + 1) & (LANES - 1)))
        inv_low = 1.0 / (odd - even)
        inv_high = 1.0 / (after - odd)
        inv_last = 1.0 / (16.0 - last)
        tables += [(even, spread(even))] * len(values)
        all_values += values
        rest += [(odd, inv_low, inv_high, last, inv_last, write) for write in writes]
    pairs = search_pairs(tables, all_values)
    knots = [lane_take(item[0], pair) for item, pair in zip(rest, pairs)]
    lows = [lane_take(item[1], pair) for item, pair in zip(rest, pairs)]
    highs = [lane_take(item[2], pair) for item, pair in zip(rest, pairs)]
    for item, value, pair, knot, low, high in zip(rest, all_values, pairs, knots, lows, highs):
        last, inv_last, write = item[3:]
        inside = (2 * pair + 1).astype(jnp.float32) + (value - knot) * jnp.where(value >= knot, high, low)
        write(jnp.where(value >= last, 256.0 + (value - last) * inv_last, inside))


def place_kernel(moves, cuts_ref, values_ref, *out_refs):
    wide = out_refs[0].shape[1]
    place_blocks([owner(move) * wide for move in moves], cuts_ref, values_ref, out_refs)


def place_blocks(bases, cuts_ref, values_ref, out_refs):
    feats, wide = out_refs[0].shape
    together = 8 // len(bases)

    def store(out_ref, at, part):
        def write(value):
            out_ref[at, part : part + LANES] = value

        return write

    def step(index, carry):
        groups = []
        for turn in range(together):
            at = pl.ds(pl.multiple_of((index * together + turn) * 8, 8), 8)
            values, writes = [], []
            for base, out_ref in zip(bases, out_refs):
                for part in range(0, wide, LANES):
                    values.append(values_ref[at, pl.ds(pl.multiple_of(base + part, LANES), LANES)])
                    writes.append(store(out_ref, at, part))
            groups.append((cuts_ref[at, :LANES], cuts_ref[at, LANES:], values, writes))
        place_groups(groups)
        return carry

    lax.fori_loop(0, feats // (8 * together), step, 0)


def place(moves, cuts, values):
    feats, rows = values.shape
    block = jax.ShapeDtypeStruct((feats, rows // 8), jnp.float32)
    return pl.pallas_call(
        lambda *refs: place_kernel(moves, *refs),
        in_specs=in_vmem(2),
        out_specs=in_vmem(len(moves)),
        out_shape=[block] * len(moves),
        compiler_params=pltpu.CompilerParams(vmem_limit_bytes=16 << 20),
        cost_estimate=pl.CostEstimate(flops=10**5, bytes_accessed=10**4, transcendentals=0),
        name="place",
    )(cuts, values)


def far_kernel(far_ref, core_ref, *refs):
    feats = far_ref.shape[0]
    cuts_refs = [far_ref, core_ref.at[:feats, :], core_ref.at[feats:, :]]
    for cuts_ref, values_ref, out_ref in zip(cuts_refs, refs[:3], refs[3:]):
        place_blocks([0], cuts_ref, values_ref, [out_ref])


def place_far(far_cuts, core_cuts, values):
    return pl.pallas_call(
        far_kernel,
        in_specs=in_vmem(2 + len(values)),
        out_specs=in_vmem(len(values)),
        out_shape=[jax.ShapeDtypeStruct(block.shape, jnp.float32) for block in values],
        compiler_params=pltpu.CompilerParams(vmem_limit_bytes=16 << 20),
        cost_estimate=pl.CostEstimate(flops=10**5, bytes_accessed=10**4, transcendentals=0),
        name="far",
    )(far_cuts, core_cuts, *values)


def join_kernel(moves, *refs):
    *parts, out_ref, sems = refs
    feats = parts[0].shape[0]
    copies = []
    for index, (move, part) in enumerate(zip(moves, parts)):
        rows = pl.ds(pl.multiple_of(owner((-move[0], move[1])) * feats, feats), feats)
        copies.append(pltpu.make_async_copy(part, out_ref.at[rows, :], sems.at[index]))
    for copy in copies:
        copy.start()
    for copy in copies:
        copy.wait()


def join(moves, parts):
    feats, wide = parts[0].shape
    return pl.pallas_call(
        lambda *refs: join_kernel(moves, *refs),
        in_specs=in_vmem(len(parts)),
        out_specs=pl.BlockSpec(memory_space=pl.ANY),
        out_shape=jax.ShapeDtypeStruct((len(parts) * feats, wide), jnp.float32),
        scratch_shapes=[pltpu.SemaphoreType.DMA((len(parts),))],
        compiler_params=pltpu.CompilerParams(vmem_limit_bytes=4 << 20),
        name="join",
    )(*parts)


def owner(move):
    me = lax.axis_index("feat")
    return (me // 2 + move[0] + 4) % 4 * 2 + (me % 2 ^ move[1])


def send_feat(array, move):
    return lax.ppermute(array, "feat", [(i, (i // 2 + move[0]) % 4 * 2 + (i % 2 ^ move[1])) for i in range(8)])


def flip_feat(array, flip):
    return lax.ppermute(array, "feat", [(i, i ^ flip) for i in range(8)])


def shift_rows(array, shift):
    return lax.ppermute(array, "rows", [(i, i // 8 * 8 + (i + shift) % 8) for i in range(32)])


def turn_rows(array, turn):
    return lax.ppermute(array, "rows", [(i, (i + 8 * turn) % 32) for i in range(32)])


def on_device(feature_values, hessian_codes, edge_codes, cut_ranks):
    hess = factor_weights(hessian_codes.reshape(-1, LANES))
    far_moves = [(2, 0), (2, 1), (0, 1)]
    codes, slots = edge_codes, []
    for flip, groups in ((1, (0,)), (2, (1,)), (4, (2, 3))):
        other = flip_feat(hess, flip)
        if flip == 1:
            top, low, *far_blocks = find_slots(0, far_moves, codes, feature_values)
            slots += [top, low]
        else:
            slots += find_near_slots(groups, codes, feature_values)
        hess = jnp.concatenate([hess, other], axis=0)
        if flip < 4:
            hess, slots, codes = lax.optimization_barrier((hess, slots, codes))
    far_blocks, hess = lax.optimization_barrier((far_blocks, hess))
    far_values = [send_feat(block, move) for block, move in zip(far_blocks, far_moves)]
    mass = find_mass(hess, slots)
    mass, far_values[2] = lax.optimization_barrier((mass, far_values[2]))
    before = mass + shift_rows(mass, 1)
    around = before + shift_rows(mass, -1)
    mass = around + shift_rows(around, -3) + shift_rows(before, 2)
    cuts = find_cuts(edge_codes, cut_ranks, mass, *[turn_rows(mass, turn) for turn in (1, 2, 3)])
    cuts, far_values = lax.optimization_barrier((cuts, far_values))
    far_cuts, moves, parts = send_feat(cuts, (2, 0)), [], []
    for index, stage in enumerate(((0, 0), (1, 0), (3, 0), (1, 1), (3, 1))):
        (out,) = place([stage], cuts, feature_values)
        cuts, out = lax.optimization_barrier((cuts, out))
        if index == 2:
            cuts, far_cuts = lax.optimization_barrier((cuts, far_cuts))
            core_cuts = send_feat(jnp.concatenate([far_cuts, cuts], axis=0), (0, 1))
        elif index == 3:
            cuts, parts[1] = lax.optimization_barrier((cuts, parts[1]))
        elif index == 4:
            cuts, far_values, parts[2] = lax.optimization_barrier((cuts, far_values, parts[2]))
        moves.append(stage)
        parts.append(send_feat(out, stage) if stage != (0, 0) else out)
    return join(moves + far_moves, parts + list(place_far(far_cuts, core_cuts, far_values)))


def solution(mesh):
    placed = (P("feat", "rows"), P(("rows", "feat")), P("feat", None), P("feat", None))
    return jax.shard_map(
        on_device, mesh=mesh, in_specs=placed, out_specs=P(None, ("rows", "feat")), check_vma=False
    )
```

```python
import jax
import jax.numpy as jnp
from jax import lax
from jax.experimental import pallas as pl
from jax.experimental.pallas import tpu as pltpu
from jax.sharding import PartitionSpec as P

LANES = 128
FEATS = 16
DEPTH = 4
TILE = 256
UNROLL = 8


def in_vmem(count):
    return [pl.BlockSpec(memory_space=pltpu.VMEM)] * count


def lane_take(table, index):
    return jnp.take_along_axis(table, index, axis=1, mode="promise_in_bounds")


def pick_columns(wide, index):
    low = lane_take(wide[:, :LANES], index & (LANES - 1))
    high = lane_take(wide[:, LANES:], index & (LANES - 1))
    return jnp.where(index < LANES, low, high)


def lane_iota(shape):
    return lax.broadcasted_iota(jnp.int32, shape, 1)


def choose(marks, low, high, masks):
    middle = (low + high) // 2
    if not masks:
        return marks[middle]
    upper = choose(marks, middle, high, masks[1:])
    return jnp.where(masks[0], upper, choose(marks, low, middle, masks[1:]))


def spread(even):
    return {i: jnp.broadcast_to(even[:, i : i + 1], even.shape) for i in range(128 >> DEPTH, 128, 128 >> DEPTH)}


def search_pairs(tables, values):
    masks = [[] for _ in values]
    for _ in range(DEPTH):
        for (_, marks), mask, value in zip(tables, masks, values):
            mask.append(value >= choose(marks, 0, LANES, mask))
    bases = []
    for mask in masks:
        base = jnp.where(mask[0], 64, 0)
        for level in range(1, DEPTH):
            base = base + jnp.where(mask[level], 64 >> level, 0)
        bases.append(base)
    step = 64 >> DEPTH
    while step:
        probes = [base + step for base in bases]
        entries = [lane_take(even, probe) for (even, _), probe in zip(tables, probes)]
        bases = [jnp.where(v >= e, p, b) for v, e, p, b in zip(values, entries, probes, bases)]
        step //= 2
    return bases


def even_odd(codes):
    lane = lane_iota((codes.shape[0], LANES))
    edges = codes.astype(jnp.float32) * (1.0 / 256.0)
    return pick_columns(edges, 2 * lane), pick_columns(edges, 2 * lane + 1)


def slot_kernel(group, moves, codes_hbm, values_hbm, top_ref, low_ref, *refs):
    *blocks, codes_ref, values_ref, sems = refs
    rows = values_ref.shape[1]
    wide = blocks[0].shape[1]
    own = slice(group * FEATS, (group + 1) * FEATS)
    span = rows // 2
    copies = [pltpu.make_async_copy(codes_hbm.at[own, :], codes_ref, sems.at[2])]
    for part in range(2):
        at = slice(part * span, (part + 1) * span)
        copies.append(pltpu.make_async_copy(values_hbm.at[own, at], values_ref.at[:, at], sems.at[part]))
    for index, (move, block) in enumerate(zip(moves, blocks)):
        at = pl.ds(pl.multiple_of(owner(move) * wide, wide), wide)
        copies.append(pltpu.make_async_copy(values_hbm.at[:, at], block, sems.at[3 + index]))
    for copy in copies:
        copy.start()
    copies[0].wait()
    for part in range(2):
        copies[1 + part].wait()
        search_slots(0, codes_ref, values_ref, top_ref, low_ref, (part / 2, (part + 1) / 2))
    for copy in copies[3:]:
        copy.wait()


def search_slots(first, codes_ref, values_ref, top_ref, low_ref, share):
    width = 32
    steps = values_ref.shape[1] // (width * LANES)
    tables = []
    for half in range(2):
        at = pl.ds(first + 8 * half, 8)
        even, odd = even_odd(codes_ref[at, :])
        tables.append((at, odd, (even, spread(even))))

    def chunk(step, carry):
        columns = [pl.ds(pl.multiple_of((step * width + part) * LANES, LANES), LANES) for part in range(width)]
        tops, lows = [[] for _ in columns], [[] for _ in columns]
        for at, odd, table in tables:
            values = [values_ref[at, column] for column in columns]
            pairs = search_pairs([table] * width, values)
            entries = [lane_take(odd, pair) for pair in pairs]
            for top, low, value, pair, entry in zip(tops, lows, values, pairs, entries):
                top.append((pair >> 3).astype(jnp.float32))
                low.append((2 * (pair & 7) + jnp.where(value >= entry, 1, 0)).astype(jnp.float32))
        for column, top, low in zip(columns, tops, lows):
            top_ref[:, column] = jnp.concatenate(top, axis=0).astype(jnp.bfloat16)
            low_ref[:, column] = jnp.concatenate(low, axis=0).astype(jnp.bfloat16)
        return carry

    lax.fori_loop(int(share[0] * steps), int(share[1] * steps), chunk, 0)


def near_slot_kernel(groups, codes_ref, values_ref, *refs):
    for index, group in enumerate(groups):
        search_slots(group * FEATS, codes_ref, values_ref, *refs[2 * index : 2 * index + 2], (0, 1))


def find_near_slots(groups, edge_codes, values):
    slots = jax.ShapeDtypeStruct((FEATS, values.shape[1]), jnp.bfloat16)
    return pl.pallas_call(
        lambda *refs: near_slot_kernel(groups, *refs),
        in_specs=in_vmem(2),
        out_specs=in_vmem(2 * len(groups)),
        out_shape=[slots] * (2 * len(groups)),
        compiler_params=pltpu.CompilerParams(vmem_limit_bytes=16 << 20),
        cost_estimate=pl.CostEstimate(flops=10**7, bytes_accessed=10**7, transcendentals=0),
        name="slots",
    )(edge_codes, values)


def find_slots(group, moves, edge_codes, values):
    feats, rows = values.shape
    slots = jax.ShapeDtypeStruct((FEATS, rows), jnp.bfloat16)
    block = jax.ShapeDtypeStruct((feats, rows // 8), jnp.float32)
    return pl.pallas_call(
        lambda *refs: slot_kernel(group, moves, *refs),
        in_specs=[pl.BlockSpec(memory_space=pltpu.HBM)] * 2,
        out_specs=in_vmem(2 + len(moves)),
        out_shape=[slots] * 2 + [block] * len(moves),
        scratch_shapes=[
            pltpu.VMEM((FEATS, 256), jnp.int32),
            pltpu.VMEM((FEATS, rows), jnp.float32),
            pltpu.SemaphoreType.DMA((3 + len(moves),)),
        ],
        compiler_params=pltpu.CompilerParams(vmem_limit_bytes=16 << 20),
        cost_estimate=pl.CostEstimate(flops=10**7, bytes_accessed=10**7, transcendentals=0),
        name="slots",
    )(
        pltpu.with_memory_space_constraint(edge_codes, pltpu.HBM),
        pltpu.with_memory_space_constraint(values, pltpu.HBM),
    )


def factor_kernel(codes_hbm, out_ref, codes_ref, sem):
    copy = pltpu.make_async_copy(codes_hbm, codes_ref, sem)
    copy.start()
    copy.wait()
    weight = codes_ref[...].astype(jnp.float32)
    first = jnp.ones_like(weight)
    second = weight.astype(jnp.bfloat16).astype(jnp.float32)
    error = jnp.abs(second - weight)
    for index in range(1, 128):
        left = 1.0 + index / 128.0
        right = (weight * (1.0 / left)).astype(jnp.bfloat16).astype(jnp.float32)
        off = jnp.abs(left * right - weight)
        better = off < error
        error = jnp.minimum(off, error)
        first = jnp.where(better, left, first)
        second = jnp.where(better, right, second)
    out_ref[0] = first
    out_ref[1] = second * (1.0 / 65536.0)


def factor_weights(codes):
    return pl.pallas_call(
        factor_kernel,
        in_specs=[pl.BlockSpec(memory_space=pltpu.HBM)],
        out_specs=in_vmem(1)[0],
        out_shape=jax.ShapeDtypeStruct((2,) + codes.shape, jnp.float32),
        scratch_shapes=[pltpu.VMEM(codes.shape, jnp.int32), pltpu.SemaphoreType.DMA],
        compiler_params=pltpu.CompilerParams(vmem_limit_bytes=4 << 20),
        name="factor",
    )(pltpu.with_memory_space_constraint(codes, pltpu.HBM))


def hist_kernel(hess_ref, *refs):
    *slots, mass_ref, first_ref, second_ref, sum_ref = refs
    blocks, tiles, lanes = hess_ref.shape
    wide = tiles * lanes
    me = lax.axis_index("feat")
    for block in range(blocks // 2):
        for tile in range(tiles):
            own = pl.ds(pl.multiple_of((block ^ me) * wide + tile * lanes, lanes), lanes)
            for ref, part in ((first_ref, 0), (second_ref, 1)):
                row = hess_ref[2 * block + part, tile : tile + 1, :]
                ref[:, own] = jnp.broadcast_to(row, (FEATS, lanes)).astype(jnp.bfloat16)

    for group in range(len(slots) // 2):
        hist_group(group, *slots[2 * group : 2 * group + 2], mass_ref, first_ref, second_ref, sum_ref)


def hist_group(group, top_ref, low_ref, mass_ref, first_ref, second_ref, sum_ref):
    rows = top_ref.shape[1]
    shape = (FEATS, LANES)
    lane = lane_iota(shape)
    feat = lax.broadcasted_iota(jnp.int32, shape, 0)

    def multiply(*sums):
        zero = jnp.zeros((FEATS, TILE), jnp.bfloat16)
        units = (sums[:16], sums[16:])

        def step(index, carry):
            for turn in range(UNROLL):
                spots = [pl.ds(pl.multiple_of(((index * UNROLL + turn) * 2 + unit) * TILE, TILE), TILE) for unit in range(2)]
                for unit, at in enumerate(spots):
                    low, second = low_ref[:, at], second_ref[:, at]
                    below = jnp.concatenate([jnp.where(low <= k, second, zero) for k in range(16)], axis=0)
                    pltpu.matmul_push_rhs(below, turn % 2, unit, transpose=True)
                for unit, at in enumerate(spots):
                    top, first = top_ref[:, at], first_ref[:, at]
                    for k in range(16):
                        weighted = jnp.where(top == k, first, zero)
                        pltpu.matmul_acc_lhs(units[unit][k], weighted, load_staged_rhs=turn % 2 if k == 0 else None)
            return carry

        lax.fori_loop(0, rows // (2 * TILE * UNROLL), step, 0)
        for k in range(16):
            sum_ref[k * FEATS : (k + 1) * FEATS] = pltpu.matmul_pop(units[0][k]) + pltpu.matmul_pop(units[1][k])

    pl.run_scoped(multiply, *[pltpu.ACC(mxu_id=unit)((FEATS, TILE), jnp.float32) for unit in range(2) for _ in range(16)])

    points = [2 * lane - 1, 2 * lane]
    columns = [(point & 7) * FEATS + feat for point in points]
    results = [jnp.zeros(shape, jnp.float32)] * 2
    before = jnp.zeros(shape, jnp.float32)
    for k in range(16):
        block = sum_ref[k * FEATS : (k + 1) * FEATS]
        for parity, (point, column) in enumerate(zip(points, columns)):
            here = jnp.where((point & 15) < 8, lane_take(block[:, :LANES], column), lane_take(block[:, LANES:], column))
            results[parity] = jnp.where((point >> 4) == k, before + here, results[parity])
        before = before + lane_take(block[:, LANES:], 7 * FEATS + feat)
    own = slice(group * FEATS, (group + 1) * FEATS)
    mass_ref[own, :LANES] = results[0]
    mass_ref[own, LANES:] = results[1]


def find_mass(hess, slots):
    rows = slots[0].shape[1]
    feats = FEATS * len(slots) // 2
    return pl.pallas_call(
        hist_kernel,
        in_specs=in_vmem(1 + len(slots)),
        out_specs=in_vmem(1)[0],
        out_shape=jax.ShapeDtypeStruct((feats, 256), jnp.float32),
        scratch_shapes=[pltpu.VMEM((FEATS, rows), jnp.bfloat16)] * 2
        + [pltpu.VMEM((16 * FEATS, TILE), jnp.float32)],
        compiler_params=pltpu.CompilerParams(vmem_limit_bytes=24 << 20),
        cost_estimate=pl.CostEstimate(flops=4 * 10**9, bytes_accessed=10**7, transcendentals=0),
        name="hist",
    )(hess, *slots)


def cuts_kernel(codes_ref, ranks_ref, *refs):
    *mass_refs, cuts_ref = refs

    together = 32

    def step(group, carry):
        at = pl.ds(pl.multiple_of(group * together, together), together)
        mass = mass_refs[0][at, :]
        for mass_ref in mass_refs[1:]:
            mass = mass + mass_ref[at, :]
        cut_group(at, codes_ref, ranks_ref, mass, cuts_ref)
        return carry

    lax.fori_loop(0, codes_ref.shape[0] // together, step, 0)


def cut_group(at, codes_ref, ranks_ref, mass, cuts_ref):
    shape = (mass.shape[0], LANES)
    lane = lane_iota(shape)
    edge_even, edge_odd = even_odd(codes_ref[at, :])
    edge_next = lane_take(edge_even, (lane + 1) & (LANES - 1))
    mass_even, mass_odd = mass[:, :LANES], mass[:, LANES:]
    mass_next = lane_take(mass_even, (lane + 1) & (LANES - 1))
    total = jnp.broadcast_to(mass_odd[:, LANES - 1 :], shape)
    ranks = ranks_ref[at, :].astype(jnp.float32)
    orders = [jnp.where(lane == 0, 255, 2 * lane - 1), 2 * lane]
    targets = [pick_columns(ranks, order) * (1.0 / 65792.0) * total for order in orders]
    pairs = search_pairs([(mass_even, spread(mass_even))] * 2, targets)
    for side, (target, pair) in enumerate(zip(targets, pairs)):
        mid_mass = lane_take(mass_odd, pair)
        mid_edge = lane_take(edge_odd, pair)
        above = target >= mid_mass
        low_mass = jnp.where(above, mid_mass, lane_take(mass_even, pair))
        high_mass = jnp.where(above, lane_take(mass_next, pair), mid_mass)
        low_edge = jnp.where(above, mid_edge, lane_take(edge_even, pair))
        high_edge = jnp.where(above, lane_take(edge_next, pair), mid_edge)
        part = (target - low_mass) / (high_mass - low_mass)
        cuts_ref[at, side * LANES : (side + 1) * LANES] = low_edge + part * (high_edge - low_edge)


def find_cuts(edge_codes, cut_ranks, *sums):
    return pl.pallas_call(
        cuts_kernel,
        in_specs=in_vmem(2 + len(sums)),
        out_specs=in_vmem(1)[0],
        out_shape=jax.ShapeDtypeStruct((edge_codes.shape[0], 256), jnp.float32),
        compiler_params=pltpu.CompilerParams(vmem_limit_bytes=4 << 20),
        name="cuts",
    )(edge_codes, cut_ranks, *sums)


def place_groups(groups):
    tables, all_values, rest = [], [], []
    for raw, odd, values, writes in groups:
        shape = odd.shape
        lane = lane_iota(shape)
        last = jnp.broadcast_to(raw[:, :1], shape)
        even = jnp.where(lane == 0, -16.0, raw)
        after = jnp.where(lane == LANES - 1, last, lane_take(even, (lane + 1) & (LANES - 1)))
        inv_low = 1.0 / (odd - even)
        inv_high = 1.0 / (after - odd)
        inv_last = 1.0 / (16.0 - last)
        tables += [(even, spread(even))] * len(values)
        all_values += values
        rest += [(odd, inv_low, inv_high, last, inv_last, write) for write in writes]
    pairs = search_pairs(tables, all_values)
    knots = [lane_take(item[0], pair) for item, pair in zip(rest, pairs)]
    lows = [lane_take(item[1], pair) for item, pair in zip(rest, pairs)]
    highs = [lane_take(item[2], pair) for item, pair in zip(rest, pairs)]
    for item, value, pair, knot, low, high in zip(rest, all_values, pairs, knots, lows, highs):
        last, inv_last, write = item[3:]
        inside = (2 * pair + 1).astype(jnp.float32) + (value - knot) * jnp.where(value >= knot, high, low)
        write(jnp.where(value >= last, 256.0 + (value - last) * inv_last, inside))


def place_kernel(moves, cuts_ref, values_ref, *out_refs):
    wide = out_refs[0].shape[1]
    place_blocks([owner(move) * wide for move in moves], cuts_ref, values_ref, out_refs)


def place_blocks(bases, cuts_ref, values_ref, out_refs):
    feats, wide = out_refs[0].shape
    together = 8 // len(bases)

    def store(out_ref, at, part):
        def write(value):
            out_ref[at, part : part + LANES] = value

        return write

    def step(index, carry):
        groups = []
        for turn in range(together):
            at = pl.ds(pl.multiple_of((index * together + turn) * 8, 8), 8)
            values, writes = [], []
            for base, out_ref in zip(bases, out_refs):
                for part in range(0, wide, LANES):
                    values.append(values_ref[at, pl.ds(pl.multiple_of(base + part, LANES), LANES)])
                    writes.append(store(out_ref, at, part))
            groups.append((cuts_ref[at, :LANES], cuts_ref[at, LANES:], values, writes))
        place_groups(groups)
        return carry

    lax.fori_loop(0, feats // (8 * together), step, 0)


def place(moves, cuts, values):
    feats, rows = values.shape
    block = jax.ShapeDtypeStruct((feats, rows // 8), jnp.float32)
    return pl.pallas_call(
        lambda *refs: place_kernel(moves, *refs),
        in_specs=in_vmem(2),
        out_specs=in_vmem(len(moves)),
        out_shape=[block] * len(moves),
        compiler_params=pltpu.CompilerParams(vmem_limit_bytes=16 << 20),
        cost_estimate=pl.CostEstimate(flops=10**5, bytes_accessed=10**4, transcendentals=0),
        name="place",
    )(cuts, values)


def far_kernel(*refs):
    count = len(refs) // 3
    for cuts_ref, values_ref, out_ref in zip(refs[:count], refs[count : 2 * count], refs[2 * count :]):
        place_blocks([0], cuts_ref, values_ref, [out_ref])


def place_far(cuts, values):
    return pl.pallas_call(
        far_kernel,
        in_specs=in_vmem(2 * len(cuts)),
        out_specs=in_vmem(len(cuts)),
        out_shape=[jax.ShapeDtypeStruct(block.shape, jnp.float32) for block in values],
        compiler_params=pltpu.CompilerParams(vmem_limit_bytes=16 << 20),
        cost_estimate=pl.CostEstimate(flops=10**5, bytes_accessed=10**4, transcendentals=0),
        name="far",
    )(*cuts, *values)


def join_kernel(moves, *refs):
    *parts, out_ref, sems = refs
    feats = parts[0].shape[0]
    copies = []
    for index, (move, part) in enumerate(zip(moves, parts)):
        rows = pl.ds(pl.multiple_of(owner((-move[0], move[1])) * feats, feats), feats)
        copies.append(pltpu.make_async_copy(part, out_ref.at[rows, :], sems.at[index]))
    for copy in copies:
        copy.start()
    for copy in copies:
        copy.wait()


def join(moves, parts):
    feats, wide = parts[0].shape
    return pl.pallas_call(
        lambda *refs: join_kernel(moves, *refs),
        in_specs=in_vmem(len(parts)),
        out_specs=pl.BlockSpec(memory_space=pl.ANY),
        out_shape=jax.ShapeDtypeStruct((len(parts) * feats, wide), jnp.float32),
        scratch_shapes=[pltpu.SemaphoreType.DMA((len(parts),))],
        compiler_params=pltpu.CompilerParams(vmem_limit_bytes=4 << 20),
        name="join",
    )(*parts)


def owner(move):
    me = lax.axis_index("feat")
    return (me // 2 + move[0] + 4) % 4 * 2 + (me % 2 ^ move[1])


def send_feat(array, move):
    return lax.ppermute(array, "feat", [(i, (i // 2 + move[0]) % 4 * 2 + (i % 2 ^ move[1])) for i in range(8)])


def flip_feat(array, flip):
    return lax.ppermute(array, "feat", [(i, i ^ flip) for i in range(8)])


def shift_rows(array, shift):
    return lax.ppermute(array, "rows", [(i, i // 8 * 8 + (i + shift) % 8) for i in range(32)])


def turn_rows(array, turn):
    return lax.ppermute(array, "rows", [(i, (i + 8 * turn) % 32) for i in range(32)])


def on_device(feature_values, hessian_codes, edge_codes, cut_ranks):
    hess = factor_weights(hessian_codes.reshape(-1, LANES))
    far_moves = [(2, 0), (2, 1), (0, 1)]
    codes, slots = edge_codes, []
    for flip, groups in ((1, (0,)), (2, (1,)), (4, (2, 3))):
        other = flip_feat(hess, flip)
        if flip == 1:
            top, low, *far_blocks = find_slots(0, far_moves, codes, feature_values)
            slots += [top, low]
        else:
            slots += find_near_slots(groups, codes, feature_values)
        hess = jnp.concatenate([hess, other], axis=0)
        if flip < 4:
            hess, slots, codes = lax.optimization_barrier((hess, slots, codes))
    far_blocks, hess = lax.optimization_barrier((far_blocks, hess))
    far_values = [send_feat(block, move) for block, move in zip(far_blocks, far_moves)]
    mass = find_mass(hess, slots)
    mass, far_values[2] = lax.optimization_barrier((mass, far_values[2]))
    before = mass + shift_rows(mass, 1)
    around = before + shift_rows(mass, -1)
    mass = around + shift_rows(around, -3) + shift_rows(before, 2)
    cuts = find_cuts(edge_codes, cut_ranks, mass, *[turn_rows(mass, turn) for turn in (1, 2, 3)])
    cuts, far_values = lax.optimization_barrier((cuts, far_values))
    far_cuts, moves, parts = send_feat(cuts, (2, 0)), [], []
    for index, stage in enumerate(((0, 0), (1, 0), (3, 0), (1, 1), (3, 1))):
        (out,) = place([stage], cuts, feature_values)
        cuts, out = lax.optimization_barrier((cuts, out))
        if index == 2:
            cuts, far_cuts = lax.optimization_barrier((cuts, far_cuts))
            core_cuts = send_feat(jnp.concatenate([far_cuts, cuts], axis=0), (0, 1))
        elif index == 3:
            cuts, parts[1] = lax.optimization_barrier((cuts, parts[1]))
        elif index == 4:
            cuts, far_values, parts[2] = lax.optimization_barrier((cuts, far_values, parts[2]))
        moves.append(stage)
        parts.append(send_feat(out, stage) if stage != (0, 0) else out)
    feats = cuts.shape[0]
    cuts_there = [far_cuts, core_cuts[:feats], core_cuts[feats:]]
    return join(moves + far_moves, parts + list(place_far(cuts_there, far_values)))


def solution(mesh):
    placed = (P("feat", "rows"), P(("rows", "feat")), P("feat", None), P("feat", None))
    return jax.shard_map(
        on_device, mesh=mesh, in_specs=placed, out_specs=P(None, ("rows", "feat")), check_vma=False
    )
```

```python
import jax
import jax.numpy as jnp
from jax import lax
from jax.experimental import pallas as pl
from jax.experimental.pallas import tpu as pltpu
from jax.sharding import PartitionSpec as P

LANES = 128
FEATS = 16
DEPTH = 4
TILE = 256
UNROLL = 8


def in_vmem(count):
    return [pl.BlockSpec(memory_space=pltpu.VMEM)] * count


def lane_take(table, index):
    return jnp.take_along_axis(table, index, axis=1, mode="promise_in_bounds")


def pick_columns(wide, index):
    low = lane_take(wide[:, :LANES], index & (LANES - 1))
    high = lane_take(wide[:, LANES:], index & (LANES - 1))
    return jnp.where(index < LANES, low, high)


def lane_iota(shape):
    return lax.broadcasted_iota(jnp.int32, shape, 1)


def choose(marks, low, high, masks):
    middle = (low + high) // 2
    if not masks:
        return marks[middle]
    upper = choose(marks, middle, high, masks[1:])
    return jnp.where(masks[0], upper, choose(marks, low, middle, masks[1:]))


def spread(even):
    return {i: jnp.broadcast_to(even[:, i : i + 1], even.shape) for i in range(128 >> DEPTH, 128, 128 >> DEPTH)}


def search_pairs(tables, values):
    masks = [[] for _ in values]
    for _ in range(DEPTH):
        for (_, marks), mask, value in zip(tables, masks, values):
            mask.append(value >= choose(marks, 0, LANES, mask))
    bases = []
    for mask in masks:
        base = jnp.where(mask[0], 64, 0)
        for level in range(1, DEPTH):
            base = base + jnp.where(mask[level], 64 >> level, 0)
        bases.append(base)
    step = 64 >> DEPTH
    while step:
        probes = [base + step for base in bases]
        entries = [lane_take(even, probe) for (even, _), probe in zip(tables, probes)]
        bases = [jnp.where(v >= e, p, b) for v, e, p, b in zip(values, entries, probes, bases)]
        step //= 2
    return bases


def even_odd(codes):
    lane = lane_iota((codes.shape[0], LANES))
    edges = codes.astype(jnp.float32) * (1.0 / 256.0)
    return pick_columns(edges, 2 * lane), pick_columns(edges, 2 * lane + 1)


def slot_kernel(group, moves, codes_hbm, values_hbm, top_ref, low_ref, *refs):
    *blocks, codes_ref, values_ref, sems = refs
    rows = values_ref.shape[1]
    wide = blocks[0].shape[1]
    own = slice(group * FEATS, (group + 1) * FEATS)
    span = rows // 2
    copies = [pltpu.make_async_copy(codes_hbm.at[own, :], codes_ref, sems.at[2])]
    for part in range(2):
        at = slice(part * span, (part + 1) * span)
        copies.append(pltpu.make_async_copy(values_hbm.at[own, at], values_ref.at[:, at], sems.at[part]))
    for index, (move, block) in enumerate(zip(moves, blocks)):
        at = pl.ds(pl.multiple_of(owner(move) * wide, wide), wide)
        copies.append(pltpu.make_async_copy(values_hbm.at[:, at], block, sems.at[3 + index]))
    for copy in copies:
        copy.start()
    copies[0].wait()
    for part in range(2):
        copies[1 + part].wait()
        search_slots(0, codes_ref, values_ref, top_ref, low_ref, (part / 2, (part + 1) / 2))
    for copy in copies[3:]:
        copy.wait()


def search_slots(first, codes_ref, values_ref, top_ref, low_ref, share):
    width = 32
    steps = values_ref.shape[1] // (width * LANES)
    tables = []
    for half in range(2):
        at = pl.ds(first + 8 * half, 8)
        even, odd = even_odd(codes_ref[at, :])
        tables.append((at, odd, (even, spread(even))))

    def chunk(step, carry):
        columns = [pl.ds(pl.multiple_of((step * width + part) * LANES, LANES), LANES) for part in range(width)]
        tops, lows = [[] for _ in columns], [[] for _ in columns]
        for at, odd, table in tables:
            values = [values_ref[at, column] for column in columns]
            pairs = search_pairs([table] * width, values)
            entries = [lane_take(odd, pair) for pair in pairs]
            for top, low, value, pair, entry in zip(tops, lows, values, pairs, entries):
                top.append((pair >> 3).astype(jnp.float32))
                low.append((2 * (pair & 7) + jnp.where(value >= entry, 1, 0)).astype(jnp.float32))
        for column, top, low in zip(columns, tops, lows):
            top_ref[:, column] = jnp.concatenate(top, axis=0).astype(jnp.bfloat16)
            low_ref[:, column] = jnp.concatenate(low, axis=0).astype(jnp.bfloat16)
        return carry

    lax.fori_loop(int(share[0] * steps), int(share[1] * steps), chunk, 0)


def near_slot_kernel(groups, codes_ref, values_ref, *refs):
    for index, group in enumerate(groups):
        search_slots(group * FEATS, codes_ref, values_ref, *refs[2 * index : 2 * index + 2], (0, 1))


def find_near_slots(groups, edge_codes, values):
    slots = jax.ShapeDtypeStruct((FEATS, values.shape[1]), jnp.bfloat16)
    return pl.pallas_call(
        lambda *refs: near_slot_kernel(groups, *refs),
        in_specs=in_vmem(2),
        out_specs=in_vmem(2 * len(groups)),
        out_shape=[slots] * (2 * len(groups)),
        compiler_params=pltpu.CompilerParams(vmem_limit_bytes=16 << 20),
        cost_estimate=pl.CostEstimate(flops=10**7, bytes_accessed=10**7, transcendentals=0),
        name="slots",
    )(edge_codes, values)


def find_slots(group, moves, edge_codes, values):
    feats, rows = values.shape
    slots = jax.ShapeDtypeStruct((FEATS, rows), jnp.bfloat16)
    block = jax.ShapeDtypeStruct((feats, rows // 8), jnp.float32)
    return pl.pallas_call(
        lambda *refs: slot_kernel(group, moves, *refs),
        in_specs=[pl.BlockSpec(memory_space=pltpu.HBM)] * 2,
        out_specs=in_vmem(2 + len(moves)),
        out_shape=[slots] * 2 + [block] * len(moves),
        scratch_shapes=[
            pltpu.VMEM((FEATS, 256), jnp.int32),
            pltpu.VMEM((FEATS, rows), jnp.float32),
            pltpu.SemaphoreType.DMA((3 + len(moves),)),
        ],
        compiler_params=pltpu.CompilerParams(vmem_limit_bytes=16 << 20),
        cost_estimate=pl.CostEstimate(flops=10**7, bytes_accessed=10**7, transcendentals=0),
        name="slots",
    )(
        pltpu.with_memory_space_constraint(edge_codes, pltpu.HBM),
        pltpu.with_memory_space_constraint(values, pltpu.HBM),
    )


def factor_kernel(codes_hbm, out_ref, codes_ref, sem):
    copy = pltpu.make_async_copy(codes_hbm, codes_ref, sem)
    copy.start()
    copy.wait()
    weight = codes_ref[...].astype(jnp.float32)
    first = jnp.ones_like(weight)
    second = weight.astype(jnp.bfloat16).astype(jnp.float32)
    error = jnp.abs(second - weight)
    for index in range(1, 128):
        left = 1.0 + index / 128.0
        right = (weight * (1.0 / left)).astype(jnp.bfloat16).astype(jnp.float32)
        off = jnp.abs(left * right - weight)
        better = off < error
        error = jnp.minimum(off, error)
        first = jnp.where(better, left, first)
        second = jnp.where(better, right, second)
    out_ref[0] = first
    out_ref[1] = second * (1.0 / 65536.0)


def factor_weights(codes):
    return pl.pallas_call(
        factor_kernel,
        in_specs=[pl.BlockSpec(memory_space=pltpu.HBM)],
        out_specs=in_vmem(1)[0],
        out_shape=jax.ShapeDtypeStruct((2,) + codes.shape, jnp.float32),
        scratch_shapes=[pltpu.VMEM(codes.shape, jnp.int32), pltpu.SemaphoreType.DMA],
        compiler_params=pltpu.CompilerParams(vmem_limit_bytes=4 << 20),
        name="factor",
    )(pltpu.with_memory_space_constraint(codes, pltpu.HBM))


def hist_kernel(hess_ref, *refs):
    *slots, mass_ref, first_ref, second_ref, sum_ref = refs
    blocks, tiles, lanes = hess_ref.shape
    wide = tiles * lanes
    me = lax.axis_index("feat")
    for block in range(blocks // 2):
        for tile in range(tiles):
            own = pl.ds(pl.multiple_of((block ^ me) * wide + tile * lanes, lanes), lanes)
            for ref, part in ((first_ref, 0), (second_ref, 1)):
                row = hess_ref[2 * block + part, tile : tile + 1, :]
                ref[:, own] = jnp.broadcast_to(row, (FEATS, lanes)).astype(jnp.bfloat16)

    for group in range(len(slots) // 2):
        hist_group(group, *slots[2 * group : 2 * group + 2], mass_ref, first_ref, second_ref, sum_ref)


def hist_group(group, top_ref, low_ref, mass_ref, first_ref, second_ref, sum_ref):
    rows = top_ref.shape[1]
    shape = (FEATS, LANES)
    lane = lane_iota(shape)
    feat = lax.broadcasted_iota(jnp.int32, shape, 0)

    def multiply(*sums):
        zero = jnp.zeros((FEATS, TILE), jnp.bfloat16)
        units = (sums[:16], sums[16:])

        def step(index, carry):
            for turn in range(UNROLL):
                spots = [pl.ds(pl.multiple_of(((index * UNROLL + turn) * 2 + unit) * TILE, TILE), TILE) for unit in range(2)]
                for unit, at in enumerate(spots):
                    low, second = low_ref[:, at], second_ref[:, at]
                    below = jnp.concatenate([jnp.where(low <= k, second, zero) for k in range(16)], axis=0)
                    pltpu.matmul_push_rhs(below, turn % 2, unit, transpose=True)
                for unit, at in enumerate(spots):
                    top, first = top_ref[:, at], first_ref[:, at]
                    for k in range(16):
                        weighted = jnp.where(top == k, first, zero)
                        pltpu.matmul_acc_lhs(units[unit][k], weighted, load_staged_rhs=turn % 2 if k == 0 else None)
            return carry

        lax.fori_loop(0, rows // (2 * TILE * UNROLL), step, 0)
        for k in range(16):
            sum_ref[k * FEATS : (k + 1) * FEATS] = pltpu.matmul_pop(units[0][k]) + pltpu.matmul_pop(units[1][k])

    pl.run_scoped(multiply, *[pltpu.ACC(mxu_id=unit)((FEATS, TILE), jnp.float32) for unit in range(2) for _ in range(16)])

    points = [2 * lane - 1, 2 * lane]
    columns = [(point & 7) * FEATS + feat for point in points]
    results = [jnp.zeros(shape, jnp.float32)] * 2
    before = jnp.zeros(shape, jnp.float32)
    for k in range(16):
        block = sum_ref[k * FEATS : (k + 1) * FEATS]
        for parity, (point, column) in enumerate(zip(points, columns)):
            here = jnp.where((point & 15) < 8, lane_take(block[:, :LANES], column), lane_take(block[:, LANES:], column))
            results[parity] = jnp.where((point >> 4) == k, before + here, results[parity])
        before = before + lane_take(block[:, LANES:], 7 * FEATS + feat)
    own = slice(group * FEATS, (group + 1) * FEATS)
    mass_ref[own, :LANES] = results[0]
    mass_ref[own, LANES:] = results[1]


def find_mass(hess, slots):
    rows = slots[0].shape[1]
    feats = FEATS * len(slots) // 2
    return pl.pallas_call(
        hist_kernel,
        in_specs=in_vmem(1 + len(slots)),
        out_specs=in_vmem(1)[0],
        out_shape=jax.ShapeDtypeStruct((feats, 256), jnp.float32),
        scratch_shapes=[pltpu.VMEM((FEATS, rows), jnp.bfloat16)] * 2
        + [pltpu.VMEM((16 * FEATS, TILE), jnp.float32)],
        compiler_params=pltpu.CompilerParams(vmem_limit_bytes=24 << 20),
        cost_estimate=pl.CostEstimate(flops=4 * 10**9, bytes_accessed=10**7, transcendentals=0),
        name="hist",
    )(hess, *slots)


def cuts_kernel(codes_ref, ranks_ref, *refs):
    *mass_refs, cuts_ref = refs

    together = 32

    def step(group, carry):
        at = pl.ds(pl.multiple_of(group * together, together), together)
        mass = mass_refs[0][at, :]
        for mass_ref in mass_refs[1:]:
            mass = mass + mass_ref[at, :]
        cut_group(at, codes_ref, ranks_ref, mass, cuts_ref)
        return carry

    lax.fori_loop(0, codes_ref.shape[0] // together, step, 0)


def cut_group(at, codes_ref, ranks_ref, mass, cuts_ref):
    shape = (mass.shape[0], LANES)
    lane = lane_iota(shape)
    edge_even, edge_odd = even_odd(codes_ref[at, :])
    edge_next = lane_take(edge_even, (lane + 1) & (LANES - 1))
    mass_even, mass_odd = mass[:, :LANES], mass[:, LANES:]
    mass_next = lane_take(mass_even, (lane + 1) & (LANES - 1))
    total = jnp.broadcast_to(mass_odd[:, LANES - 1 :], shape)
    ranks = ranks_ref[at, :].astype(jnp.float32)
    orders = [jnp.where(lane == 0, 255, 2 * lane - 1), 2 * lane]
    targets = [pick_columns(ranks, order) * (1.0 / 65792.0) * total for order in orders]
    pairs = search_pairs([(mass_even, spread(mass_even))] * 2, targets)
    for side, (target, pair) in enumerate(zip(targets, pairs)):
        mid_mass = lane_take(mass_odd, pair)
        mid_edge = lane_take(edge_odd, pair)
        above = target >= mid_mass
        low_mass = jnp.where(above, mid_mass, lane_take(mass_even, pair))
        high_mass = jnp.where(above, lane_take(mass_next, pair), mid_mass)
        low_edge = jnp.where(above, mid_edge, lane_take(edge_even, pair))
        high_edge = jnp.where(above, lane_take(edge_next, pair), mid_edge)
        part = (target - low_mass) / (high_mass - low_mass)
        cuts_ref[at, side * LANES : (side + 1) * LANES] = low_edge + part * (high_edge - low_edge)


def find_cuts(edge_codes, cut_ranks, *sums):
    return pl.pallas_call(
        cuts_kernel,
        in_specs=in_vmem(2 + len(sums)),
        out_specs=in_vmem(1)[0],
        out_shape=jax.ShapeDtypeStruct((edge_codes.shape[0], 256), jnp.float32),
        compiler_params=pltpu.CompilerParams(vmem_limit_bytes=4 << 20),
        name="cuts",
    )(edge_codes, cut_ranks, *sums)


def place_groups(groups):
    tables, all_values, rest = [], [], []
    for raw, odd, values, writes in groups:
        shape = odd.shape
        lane = lane_iota(shape)
        last = jnp.broadcast_to(raw[:, :1], shape)
        even = jnp.where(lane == 0, -16.0, raw)
        after = jnp.where(lane == LANES - 1, last, lane_take(even, (lane + 1) & (LANES - 1)))
        inv_low = 1.0 / (odd - even)
        inv_high = 1.0 / (after - odd)
        inv_last = 1.0 / (16.0 - last)
        tables += [(even, spread(even))] * len(values)
        all_values += values
        rest += [(odd, inv_low, inv_high, last, inv_last, write) for write in writes]
    pairs = search_pairs(tables, all_values)
    knots = [lane_take(item[0], pair) for item, pair in zip(rest, pairs)]
    lows = [lane_take(item[1], pair) for item, pair in zip(rest, pairs)]
    highs = [lane_take(item[2], pair) for item, pair in zip(rest, pairs)]
    for item, value, pair, knot, low, high in zip(rest, all_values, pairs, knots, lows, highs):
        last, inv_last, write = item[3:]
        inside = (2 * pair + 1).astype(jnp.float32) + (value - knot) * jnp.where(value >= knot, high, low)
        write(jnp.where(value >= last, 256.0 + (value - last) * inv_last, inside))


def place_kernel(moves, cuts_ref, values_ref, *out_refs):
    wide = out_refs[0].shape[1]
    place_blocks([owner(move) * wide for move in moves], cuts_ref, values_ref, out_refs)


def place_blocks(bases, cuts_ref, values_ref, out_refs):
    feats, wide = out_refs[0].shape
    together = 8 // len(bases)

    def store(out_ref, at, part):
        def write(value):
            out_ref[at, part : part + LANES] = value

        return write

    def step(index, carry):
        groups = []
        for turn in range(together):
            at = pl.ds(pl.multiple_of((index * together + turn) * 8, 8), 8)
            values, writes = [], []
            for base, out_ref in zip(bases, out_refs):
                for part in range(0, wide, LANES):
                    values.append(values_ref[at, pl.ds(pl.multiple_of(base + part, LANES), LANES)])
                    writes.append(store(out_ref, at, part))
            groups.append((cuts_ref[at, :LANES], cuts_ref[at, LANES:], values, writes))
        place_groups(groups)
        return carry

    lax.fori_loop(0, feats // (8 * together), step, 0)


def place(moves, cuts, values):
    feats, rows = values.shape
    block = jax.ShapeDtypeStruct((feats, rows // 8), jnp.float32)
    return pl.pallas_call(
        lambda *refs: place_kernel(moves, *refs),
        in_specs=in_vmem(2),
        out_specs=in_vmem(len(moves)),
        out_shape=[block] * len(moves),
        compiler_params=pltpu.CompilerParams(vmem_limit_bytes=16 << 20),
        cost_estimate=pl.CostEstimate(flops=10**5, bytes_accessed=10**4, transcendentals=0),
        name="place",
    )(cuts, values)


def far_kernel(*refs):
    count = len(refs) // 3
    for cuts_ref, values_ref, out_ref in zip(refs[:count], refs[count : 2 * count], refs[2 * count :]):
        place_blocks([0], cuts_ref, values_ref, [out_ref])


def place_far(cuts, values):
    return pl.pallas_call(
        far_kernel,
        in_specs=in_vmem(2 * len(cuts)),
        out_specs=in_vmem(len(cuts)),
        out_shape=[jax.ShapeDtypeStruct(block.shape, jnp.float32) for block in values],
        compiler_params=pltpu.CompilerParams(vmem_limit_bytes=16 << 20),
        cost_estimate=pl.CostEstimate(flops=10**5, bytes_accessed=10**4, transcendentals=0),
        name="far",
    )(*cuts, *values)


def join_kernel(moves, *refs):
    *parts, out_ref, sems = refs
    feats = parts[0].shape[0]
    copies = []
    for index, (move, part) in enumerate(zip(moves, parts)):
        rows = pl.ds(pl.multiple_of(owner((-move[0], move[1])) * feats, feats), feats)
        copies.append(pltpu.make_async_copy(part, out_ref.at[rows, :], sems.at[index]))
    for copy in copies:
        copy.start()
    for copy in copies:
        copy.wait()


def join(moves, parts):
    feats, wide = parts[0].shape
    return pl.pallas_call(
        lambda *refs: join_kernel(moves, *refs),
        in_specs=in_vmem(len(parts)),
        out_specs=pl.BlockSpec(memory_space=pl.ANY),
        out_shape=jax.ShapeDtypeStruct((len(parts) * feats, wide), jnp.float32),
        scratch_shapes=[pltpu.SemaphoreType.DMA((len(parts),))],
        compiler_params=pltpu.CompilerParams(vmem_limit_bytes=4 << 20),
        name="join",
    )(*parts)


def owner(move):
    me = lax.axis_index("feat")
    return (me // 2 + move[0] + 4) % 4 * 2 + (me % 2 ^ move[1])


def send_feat(array, move):
    return lax.ppermute(array, "feat", [(i, (i // 2 + move[0]) % 4 * 2 + (i % 2 ^ move[1])) for i in range(8)])


def flip_feat(array, flip):
    return lax.ppermute(array, "feat", [(i, i ^ flip) for i in range(8)])


def shift_rows(array, shift):
    return lax.ppermute(array, "rows", [(i, i // 8 * 8 + (i + shift) % 8) for i in range(32)])


def turn_rows(array, turn):
    return lax.ppermute(array, "rows", [(i, (i + 8 * turn) % 32) for i in range(32)])


def on_device(feature_values, hessian_codes, edge_codes, cut_ranks):
    hess = factor_weights(hessian_codes.reshape(-1, LANES))
    far_moves = [(2, 0), (2, 1), (0, 1)]
    codes, slots = edge_codes, []
    for flip, groups in ((1, (0,)), (2, (1,)), (4, (2, 3))):
        other = flip_feat(hess, flip)
        if flip == 1:
            top, low, *far_blocks = find_slots(0, far_moves, codes, feature_values)
            slots += [top, low]
        else:
            slots += find_near_slots(groups, codes, feature_values)
        hess = jnp.concatenate([hess, other], axis=0)
        if flip < 4:
            hess, slots, codes = lax.optimization_barrier((hess, slots, codes))
    far_blocks, hess = lax.optimization_barrier((far_blocks, hess))
    far_values = [send_feat(block, move) for block, move in zip(far_blocks, far_moves)]
    mass = find_mass(hess, slots)
    mass, far_values[2] = lax.optimization_barrier((mass, far_values[2]))
    before = mass + shift_rows(mass, 1)
    around = before + shift_rows(mass, -1)
    mass = around + shift_rows(around, -3) + shift_rows(before, 2)
    cuts = find_cuts(edge_codes, cut_ranks, mass, *[turn_rows(mass, turn) for turn in (1, 2, 3)])
    cuts, far_values = lax.optimization_barrier((cuts, far_values))
    far_cuts, moves, parts = send_feat(cuts, (2, 0)), [], []
    for index, stage in enumerate(((1, 0), (3, 0), (1, 1), (3, 1), (0, 0))):
        (out,) = place([stage], cuts, feature_values)
        cuts, out = lax.optimization_barrier((cuts, out))
        if index == 1:
            cuts, far_cuts = lax.optimization_barrier((cuts, far_cuts))
            core_cuts = send_feat(jnp.concatenate([far_cuts, cuts], axis=0), (0, 1))
        elif index == 2:
            cuts, far_values = lax.optimization_barrier((cuts, far_values))
        elif index == 3:
            cuts, parts[0] = lax.optimization_barrier((cuts, parts[0]))
        elif index == 4:
            cuts, far_values, parts[1], parts[2] = lax.optimization_barrier((cuts, far_values, parts[1], parts[2]))
        moves.append(stage)
        parts.append(send_feat(out, stage) if stage != (0, 0) else out)
    feats = cuts.shape[0]
    cuts_there = [far_cuts, core_cuts[:feats], core_cuts[feats:]]
    return join(moves + far_moves, parts + list(place_far(cuts_there, far_values)))


def solution(mesh):
    placed = (P("feat", "rows"), P(("rows", "feat")), P("feat", None), P("feat", None))
    return jax.shard_map(
        on_device, mesh=mesh, in_specs=placed, out_specs=P(None, ("rows", "feat")), check_vma=False
    )
```
